32 devices in a mesh: groups: 2 (over x), tile: 16 (over z, y, core).
Axes of the slice: x: 2, y: 2, z: 4, core: 2. Of those that a mesh axis runs over, the one named last changes fastest.
Arguments:
- tiles: float32 [2, 12288, 384], P(None, ('groups', 'tile')), parts along dimension 1, may hold values from -6 to 6
- library: float32 [128, 2, 128, 128], P('tile'), may hold values from -6 to 6
- block_owner: int32 [2], replicated, may hold values from 0 to 15
- block_clips: int32 [2, 2], replicated, may hold values from 0 to 7
- layer_order: int32 [32, 2], P(('groups', 'tile')), parts along dimension 0, may hold values from 0 to 1, each once within a row
Outputs:
- scores: float32 [2, 2, 12288, 384], P(None, None, ('groups', 'tile')), parts along dimension 2
- peak_scores: float32 [4, 2], P('groups'), parts along dimension 0
The draws below stay inside these ranges and needn't reach their ends.
There are 2 independent parts, one for each index of `groups`. The reference program is written for one: setup_inputs(seed, part) draws one part's arguments, and reference() takes and returns one part's arrays. A program takes and returns all parts, laid end to end along the dimension named above; an argument that names none is the same for every part. Nothing has to cross between parts.
Inputs may be any that keep to these rules, and one draw needn't show every extreme that they name: `layer_order`: each row is a permutation of 0 to 1.
All inputs are finite; a program needn't handle non-finite values.
Results may differ from the reference program's by a relative error of at most 0.000098.
Values sent between devices are 32-bit elements; how exact they have to be, the bound alone decides.
A program may use at most 128 MiB of HBM per device.

```python
import math
import jax
import jax.numpy as jnp
from jax import lax

SPAN = 512
CLIP = 128
LAYERS = 2
CLIPS_DEV = 8
BLOCKS = 2
PER_BLOCK = 2
ROWS = 384
COLS = 384
TILES = 16
LIBRARY = 128


def place_ends(drawn, rng, low, top_value):
    place = [jax.random.randint(jax.random.fold_in(rng, axis), (), 0, length) for axis, length in enumerate(drawn.shape)]
    main_axis = drawn.shape.index(max(drawn.shape))
    neighbour = place[:main_axis] + [(place[main_axis] + 1) % drawn.shape[main_axis]] + place[main_axis + 1:]
    return drawn.at[tuple(place)].set(low).at[tuple(neighbour)].set(top_value)


def levels(key, shape, pieces, least, top_value):
    gain, own = 1.0, jax.random.fold_in(key, 6)
    for axis_at, parts in pieces:
        steps = jnp.exp(jax.random.uniform(jax.random.fold_in(own, axis_at), (parts,), jnp.float32, least / len(pieces), top_value / len(pieces)))
        gain = gain * jnp.repeat(steps, shape[axis_at] // parts).reshape([-1 if axis == axis_at else 1 for axis in range(len(shape))])
    return gain


def centred(stream_key, shape, width, most, split=(), held_as=jnp.bfloat16):
    drawn = width * jax.random.normal(stream_key, shape, jnp.float32)
    if split:
        drawn = drawn * levels(stream_key, shape, split, -0.22, 0.18)
    return jnp.clip(drawn, -most, most).astype(held_as)


def setup_inputs(seed: int = 0, part: int = 0) -> dict:
    seeds = jax.random.split(jax.random.key(seed), 6)
    own_keys = jax.random.split(jax.random.fold_in(seeds[5], part), 6)
    return {
        "tiles": centred(own_keys[0], (LAYERS, TILES * ROWS, COLS), 1.0, 6.0, ((1, 16),), jnp.float32),
        "library": centred(seeds[1], (LIBRARY, LAYERS, CLIP, CLIP), 1.0, 6.0, ((0, 16),), jnp.float32),
        "block_owner": jax.random.randint(seeds[2], (BLOCKS,), 0, TILES).astype(jnp.int32),
        "block_clips": place_ends(jax.random.randint(seeds[3], (BLOCKS, PER_BLOCK), 0, CLIPS_DEV), jax.random.fold_in(seeds[3], 1), 0, CLIPS_DEV - 1).astype(jnp.int32),
        "layer_order": jax.vmap(lambda own: jax.random.permutation(own, LAYERS))(jax.random.split(own_keys[4], TILES)).reshape((TILES, LAYERS)).astype(jnp.int32),
    }


def window_band(length, starts, extent, number_type):
    position = jnp.arange(length)[:, None]
    anchor = jnp.arange(starts)[None, :]
    offset = position - anchor
    return ((offset >= 0) & (offset < extent)).astype(number_type)

def reference(tiles, library, block_owner, block_clips, layer_order):
    chosen = (block_owner[:, None] * CLIPS_DEV + block_clips).reshape(-1).astype(jnp.int32)
    chosen_clips = library[chosen]
    clip_rms = jnp.sqrt(lax.optimization_barrier(jnp.mean(chosen_clips * chosen_clips, axis=(1, 2, 3))) + 1e-05)
    padded_clips = jnp.pad(chosen_clips, ((0, 0), (0, 0), (0, SPAN - CLIP), (0, SPAN - CLIP)))
    clip_spectra = jnp.conj(jnp.fft.fft2(padded_clips))
    strip_rows = tiles.reshape(LAYERS, TILES, ROWS, COLS)
    following = jnp.concatenate([strip_rows[:, 1:, :CLIP, :], jnp.zeros((LAYERS, 1, CLIP, COLS), tiles.dtype)], axis=1)
    extended = jnp.moveaxis(jnp.concatenate([strip_rows, following], axis=2), 1, 0)
    band_rows = window_band(SPAN, ROWS, CLIP, tiles.dtype)
    band_cols = window_band(COLS, COLS, CLIP, tiles.dtype)
    root_count = math.sqrt(LAYERS * CLIP * CLIP)

    def one_tile(inputs):
        tile_block, layer_pick = inputs
        padded = jnp.pad(tile_block, ((0, 0), (0, 0), (0, SPAN - COLS)))
        spectra = jnp.fft.fft2(padded)
        crossed = lax.optimization_barrier(jnp.sum(spectra[None] * clip_spectra[:, layer_pick], axis=1))
        correlation = jnp.real(jnp.fft.ifft2(crossed))[:, :ROWS, :COLS]
        squares = lax.optimization_barrier(jnp.sum(tile_block * tile_block, axis=0))
        energy = jnp.dot(jnp.dot(band_rows.T, squares, precision=lax.Precision.HIGHEST), band_cols, precision=lax.Precision.HIGHEST)
        window_rms = jnp.sqrt(energy / (LAYERS * CLIP * CLIP) + 1e-05)
        return correlation / (root_count * clip_rms[:, None, None] * window_rms[None])
    all_scores = lax.map(one_tile, (extended, layer_order))
    all_scores = jnp.moveaxis(all_scores, 1, 0).reshape(BLOCKS, PER_BLOCK, TILES * ROWS, COLS)
    peak_scores = lax.optimization_barrier(jnp.max(all_scores, axis=(2, 3)))
    return (all_scores, peak_scores)
```

```python
import functools
import math

import jax
import jax.numpy as jnp
import numpy as np
from jax import lax
from jax.experimental import pallas as pl
from jax.experimental.pallas import tpu as pltpu
from jax.sharding import PartitionSpec as P

F32 = jnp.float32
BF16 = jnp.bfloat16


def split(x):
    high = x.astype(BF16)
    return high, (x - high.astype(F32)).astype(BF16)


def mm(a, b):
    return jnp.dot(a, b, preferred_element_type=F32)


def transform_matrix(extent):
    span = 2 * extent
    odd = 2 * np.arange(extent)[:, None] + 1
    angle = (odd * np.arange(span)[None, :] % (2 * span)) * (math.pi / span)
    return np.concatenate([np.cos(angle), np.sin(angle)], axis=0).astype(np.float32)


def halves(matrix):
    high = matrix.astype(BF16)
    low = (matrix - high.astype(np.float32)).astype(BF16)
    return high, low


def constants(extent):
    forward = transform_matrix(extent)
    fh, fl = halves(forward)
    row_left = np.concatenate([fh, fl, fh], axis=1)
    ft = np.ascontiguousarray(forward.T)
    th, tl = halves(ft)
    col_right = np.stack([th, tl])
    back = forward[:, :extent] * np.float32(1.0 / extent)
    bh, bl = halves(back)
    back_right = np.stack([bh, bl])
    back_left = np.concatenate([bh.T, bl.T, bh.T], axis=1)
    offset = np.arange(2 * extent)[None, :] - np.arange(extent)[:, None]
    band = ((offset >= 0) & (offset < extent)).astype(BF16)
    band_left = np.concatenate([band, band], axis=1)
    band_right = np.ascontiguousarray(band.T)
    return [jnp.asarray(c) for c in (row_left, col_right, back_left, back_right, band_left, band_right)]


def combine(y, e):
    a, b = y[:e, :e], y[:e, e:]
    c, d = y[e:, :e], y[e:, e:]
    return a - d, b + c, a + d, c - b


class Transforms:
    def __init__(self, refs, shapes):
        self.__dict__.update(refs)
        self.layers, self.rows, self.cols, self.e, self.per_block, self.count = shapes
        self.span = 2 * self.e
        self.nc = self.cols // self.e
        self.entries = self.layers * self.e * self.e

    def rows_of(self, b, window):
        e, squares = self.e, None
        for l in range(self.layers):
            x = window(l)
            squares = x * x if squares is None else squares + x * x
            xh, xl = split(x)
            y = mm(self.row_left[...], jnp.concatenate([xh, xh, xl], axis=0))
            h, low = split(y)
            self.yh[l], self.yl[l] = h, low
        sh, sl = split(squares)
        energy = mm(self.band_left[...], jnp.concatenate([sh, sl], axis=0))
        eh, el = split(energy)
        for c in range(self.nc):
            width = min(2, self.nc - c) * e
            at = slice(c * e, c * e + width)
            total = mm(eh[:, at], self.band_right[:width]) + mm(el[:, at], self.band_right[:width])
            self.inv[b, :, c * e:(c + 1) * e] = 1.0 / jnp.sqrt(total / self.entries + 1e-05)

    def columns_of(self, b):
        e = self.e
        for c in range(self.nc):
            width = min(2, self.nc - c) * e
            at = slice(c * e, c * e + width)
            for l in range(self.layers):
                h, low = self.yh[l, :, at], self.yl[l, :, at]
                y = mm(h, self.col_right[0, :width]) + mm(low, self.col_right[0, :width]) + mm(h, self.col_right[1, :width])
                for n, part in enumerate(combine(y, e)):
                    self.tile_parts[b, c, l, n] = part

    def clip_of(self, k, layer_at):
        e, span, row_left, col_right = self.e, self.span, self.row_left, self.col_right
        total = jnp.zeros((e, e), F32)
        for l in range(self.layers):
            chosen = layer_at(l)
            total = total + chosen * chosen
            ch, cl = split(chosen)
            first = mm(row_left[:, :e], ch) + mm(row_left[:, span:span + e], ch) + mm(row_left[:, :e], cl)
            fh, fl = split(first)
            second = mm(fh, col_right[0, :e]) + mm(fl, col_right[0, :e]) + mm(fh, col_right[1, :e])
            for n, part in enumerate(combine(second, e)):
                self.spectra[k, l, n] = part
        mean = jnp.sum(total, keepdims=True) / self.entries
        return 1.0 / (math.sqrt(self.entries) * jnp.sqrt(mean + 1e-05))

    def inverse_of(self, b, clip_scale):
        e = self.e
        for c in range(self.nc):
            for k in range(self.count):
                u1 = u2 = v1 = v2 = None
                for l in range(self.layers):
                    p1, p2, q1, q2 = (self.tile_parts[b, c, l, n] for n in range(4))
                    c1, c2, d1, d2 = (self.spectra[k, l, n] for n in range(4))
                    t = (p1 * c1 + p2 * c2, p2 * c1 - p1 * c2, q1 * d1 + q2 * d2, q2 * d1 - q1 * d2)
                    if u1 is None:
                        u1, u2, v1, v2 = t
                    else:
                        u1, u2, v1, v2 = u1 + t[0], u2 + t[1], v1 + t[2], v2 + t[3]
                z = jnp.concatenate([
                    jnp.concatenate([u1 + v1, u2 - v2], axis=1),
                    jnp.concatenate([u2 + v2, v1 - u1], axis=1)], axis=0)
                zh, zl = split(z)
                w = mm(zh, self.back_right[0]) + mm(zl, self.back_right[0]) + mm(zh, self.back_right[1])
                h, low = split(w)
                self.wh[k, :, c * e:(c + 1) * e] = h
                self.wl[k, :, c * e:(c + 1) * e] = low
        scale = self.inv[b]
        for k in range(self.count):
            out = mm(self.back_left[...], jnp.concatenate([self.wh[k], self.wh[k], self.wl[k]], axis=0))
            out = out * scale * (clip_scale[k] * 0.5)
            self.scores[k // self.per_block, k % self.per_block, pl.ds(pl.multiple_of(b * e, e), e)] = out
            top = jnp.max(out, axis=0, keepdims=True)
            best = self.peaks[k:k + 1]
            for c in range(self.nc):
                best = jnp.maximum(best, top[:, c * e:(c + 1) * e])
            self.peaks[k:k + 1] = best


MESH = pl.DeviceIdType.MESH
PLANE = 4
CHUNKS = 4


def kernel(tiles_n, owner, picks, order, *refs):
    sources = refs[:8]
    (scores, peak_out,
           yh, yl, inv, tile_parts, spectra, wh, wl, peaks, slots,
           stage, landed, mine, rbuf, lbuf, rsend, lsend, full, halo_in,
           rs_send, rs_recv, r_send, r_recv, l_send, l_recv,
           ag_send, ag_recv, fw_send, fw_recv, halo_send, halo_recv, peak_send, peak_recv,
           library, tiles, row_left, col_right, back_left, back_right, band_left, band_right, load_sem) = refs[8:]
    loads = [pltpu.make_async_copy(a, b, load_sem.at[n]) for n, (a, b) in enumerate(zip(
        sources, (library, tiles, row_left, col_right, back_left, back_right, band_left, band_right)))]
    for load in loads:
        load.start()
    g = lax.axis_index("groups")
    t = lax.axis_index("tile")
    per_block = picks.shape[1]
    layers, rows, cols = tiles.shape
    e = library.shape[-1]
    nr = rows // e
    count = picks.shape[0] * per_block
    work = Transforms(dict(row_left=row_left, col_right=col_right, back_left=back_left, back_right=back_right,
                           band_left=band_left, band_right=band_right, scores=scores, yh=yh, yl=yl, inv=inv,
                           tile_parts=tile_parts, spectra=spectra, wh=wh, wl=wl, peaks=peaks),
                      (layers, rows, cols, e, per_block, count))
    z = t // PLANE
    q = lax.rem(t, PLANE)
    depth = tiles_n // PLANE
    parity = lax.rem(g, 2)
    other_g = g + 1 - 2 * parity
    core = lax.rem(q, 2)
    partner = t + 1 - 2 * core
    upper = q // 2
    across = t + 2 - 4 * upper
    plane = [z * PLANE + lax.rem(q + d, PLANE) for d in range(1, PLANE)]
    others = [(g, lax.rem(t + d, tiles_n)) for d in range(1, tiles_n)]
    greeted = others + [(other_g, t), (other_g, across)]

    barrier = pltpu.get_barrier_semaphore()
    for target in greeted:
        pl.semaphore_signal(barrier, inc=1, device_id=target, device_id_type=MESH)

    loads[0].wait()

    def contribution(slab):
        clip, layer = slab // layers, lax.rem(slab, layers)
        block, which = clip // per_block, lax.rem(clip, per_block)
        mask = jnp.where(owner[block] == t, 1.0, 0.0).astype(F32)
        return library[picks[block, which], layer] * mask

    for d in range(PLANE):
        stage[d] = contribution(parity * PLANE + lax.rem(q + d, PLANE))

    @pl.when(z == 0)
    def _():
        rbuf[...] = jnp.zeros_like(rbuf)

    @pl.when(z == depth - 1)
    def _():
        lbuf[...] = jnp.zeros_like(lbuf)

    @pl.when(t == tiles_n - 1)
    def _():
        halo_in[...] = jnp.zeros_like(halo_in)

    peaks[...] = jnp.full(peaks.shape, -jnp.inf, F32)
    pl.semaphore_wait(barrier, len(greeted))

    def remote(src, dst, send, recv, target):
        return pltpu.make_async_remote_copy(src_ref=src, dst_ref=dst, send_sem=send, recv_sem=recv,
                                            device_id=target, device_id_type=MESH)

    scatter = []
    for d in range(1, PLANE):
        copy = remote(stage.at[d], landed.at[d - 1], rs_send.at[d - 1], rs_recv.at[d - 1], (g, plane[d - 1]))
        copy.start()
        scatter.append(copy)
    for load in loads[1:]:
        load.wait()
    work.rows_of(0, lambda l: tiles[l, :2 * e])
    for copy in scatter:
        copy.wait()
    mine[...] = stage[0] + landed[0] + landed[1] + landed[2]

    step = e // CHUNKS
    parts = [pl.ds(c * step, step) for c in range(CHUNKS)]
    slab = parity * PLANE + q
    right = [remote(rsend.at[c], rbuf.at[c], r_send.at[c], r_recv.at[c], (g, t + PLANE)) for c in range(CHUNKS)]
    left = [remote(lsend.at[c], lbuf.at[c], l_send.at[c], l_recv.at[c], (g, t - PLANE)) for c in range(CHUNKS)]
    forwards = []
    slabs = [slab, (1 - parity) * PLANE + q,
             parity * PLANE + q + 2 - 4 * upper, (1 - parity) * PLANE + q + 2 - 4 * upper]
    targets = [(other_g, t), (g, across), (other_g, across)]

    def forward(n, c):
        copy = remote(full.at[slabs[n], parts[c]], full.at[slabs[n], parts[c]],
                      fw_send.at[n, c], fw_recv.at[n, c], (g, partner))
        copy.start()
        forwards.append(copy)

    gathers = [(n, c, remote(full.at[slab, parts[c]], full.at[slab, parts[c]], ag_send.at[n, c], ag_recv.at[n, c], target))
               for c in range(CHUNKS) for n, target in enumerate(targets)]
    own = [remote(full.at[slab, parts[c]], full.at[slab, parts[c]], fw_send.at[0, c], fw_recv.at[0, c], (g, partner))
           for c in range(CHUNKS)]

    def rightward(c):
        @pl.when(z > 0)
        def _():
            right[c].wait_recv()
        rsend[c] = rbuf[c] + mine[parts[c]]

        @pl.when(z < depth - 1)
        def _():
            right[c].start()

    def leftward(c):
        @pl.when(z < depth - 1)
        def _():
            left[c].wait_recv()
        lsend[c] = lbuf[c] + mine[parts[c]]

        @pl.when(z > 0)
        def _():
            left[c].start()

    def deliver(c):
        full[slab, parts[c]] = rsend[c] + lbuf[c]
        for n in range(3):
            gathers[3 * c + n][2].start()
        own[c].start()

    lower = z < depth // 2
    for condition, first, second in ((lower, rightward, leftward), (jnp.logical_not(lower), leftward, rightward)):
        @pl.when(condition)
        def _(first=first, second=second):
            for c in range(CHUNKS):
                first(c)
            for c in range(CHUNKS):
                second(c)
                deliver(c)
    forwards.extend(own)
    work.columns_of(0)
    work.rows_of(1, lambda l: tiles[l, e:3 * e])
    for n, c, copy in gathers:
        copy.wait_recv()
        forward(n + 1, c)
    halo = remote(tiles.at[:, pl.ds(0, e)], halo_in, halo_send, halo_recv, (g, t - 1))

    @pl.when(t > 0)
    def _():
        halo.start()

    for b in range(1, nr - 1):
        if b > 1:
            work.rows_of(b, lambda l: tiles[l, b * e:(b + 2) * e])
        work.columns_of(b)
    for copy in forwards:
        copy.wait_recv()
    clip_scale = [work.clip_of(k, lambda l: full[k * layers + order[0, l]]) for k in range(count)]

    def row_block(b, carry):
        @pl.when(b == nr - 1)
        def _():
            @pl.when(t < tiles_n - 1)
            def _():
                halo.wait_recv()
            work.rows_of(nr - 1, lambda l: jnp.concatenate([tiles[l, rows - e:], halo_in[l]], axis=0))
            work.columns_of(nr - 1)
        work.inverse_of(b, clip_scale)
        return carry

    lax.fori_loop(0, nr, row_block, 0)

    copies = [remote(peaks, slots.at[n], peak_send.at[n], peak_recv.at[n], target) for n, target in enumerate(others)]
    for copy in copies:
        copy.start()
    for _, _, copy in gathers:
        copy.wait_send()
    for copy in forwards:
        copy.wait_send()
    for c in range(CHUNKS):
        @pl.when(z < depth - 1)
        def _(c=c):
            right[c].wait_send()

        @pl.when(z > 0)
        def _(c=c):
            left[c].wait_send()

    @pl.when(t > 0)
    def _():
        halo.wait_send()

    best = peaks[...]
    for n, copy in enumerate(copies):
        copy.wait_recv()
        best = jnp.maximum(best, slots[n])
    best = jnp.max(best, axis=1, keepdims=True)
    for k in range(count):
        at = k % per_block
        peak_out[k // per_block:k // per_block + 1, at:at + 1] = best[k:k + 1]
    for copy in copies:
        copy.wait_send()


def write_out(scores, peaks, scores_out, peaks_out, sem):
    copies = [pltpu.make_async_copy(scores, scores_out, sem.at[0]), pltpu.make_async_copy(peaks, peaks_out, sem.at[1])]
    for copy in copies:
        copy.start()
    for copy in copies:
        copy.wait()


def local(tiles, library, block_owner, block_clips, layer_order):
    layers, rows, cols = tiles.shape
    e = library.shape[-1]
    span, nr, nc = 2 * e, rows // e, cols // e
    blocks, per_block = block_clips.shape
    count = blocks * per_block
    slabs = count * layers
    assert slabs == 2 * PLANE
    tiles_n = lax.axis_size("tile")
    smem = pl.BlockSpec(memory_space=pltpu.SMEM)
    vmem = pl.BlockSpec(memory_space=pltpu.VMEM)
    dma = pltpu.SemaphoreType.DMA
    piece = pltpu.VMEM((CHUNKS, e // CHUNKS, e), F32)
    lines = -(-count // 8) * 8
    operands = [library, tiles, *constants(e)]
    scores, peaks = pl.pallas_call(
        functools.partial(kernel, tiles_n),
        out_shape=(pltpu.VMEM((blocks, per_block, rows, cols), F32),
                   pltpu.VMEM((blocks, per_block), F32)),
        in_specs=[smem] * 3 + [pl.BlockSpec(memory_space=pltpu.HBM)] * 8,
        out_specs=(vmem, vmem),
        scratch_shapes=[
            pltpu.VMEM((layers, span, cols), BF16), pltpu.VMEM((layers, span, cols), BF16),
            pltpu.VMEM((nr, e, cols), F32),
            pltpu.VMEM((nr, nc, layers, 4, e, e), F32), pltpu.VMEM((count, layers, 4, e, e), F32),
            pltpu.VMEM((count, span, cols), BF16), pltpu.VMEM((count, span, cols), BF16),
            pltpu.VMEM((lines, e), F32), pltpu.VMEM((tiles_n - 1, lines, e), F32),
            pltpu.VMEM((PLANE, e, e), F32), pltpu.VMEM((PLANE - 1, e, e), F32), pltpu.VMEM((e, e), F32),
            piece, piece, piece, piece,
            pltpu.VMEM((slabs, e, e), F32), pltpu.VMEM((layers, e, cols), F32),
            dma((PLANE - 1,)), dma((PLANE - 1,)), dma((CHUNKS,)), dma((CHUNKS,)), dma((CHUNKS,)), dma((CHUNKS,)),
            dma((3, CHUNKS)), dma((3, CHUNKS)), dma((4, CHUNKS)), dma((4, CHUNKS)), dma, dma,
            dma((tiles_n - 1,)), dma((tiles_n - 1,)),
        ] + [pltpu.VMEM(a.shape, a.dtype) for a in operands] + [dma((len(operands),))],
        compiler_params=pltpu.CompilerParams(collective_id=0, has_side_effects=True, vmem_limit_bytes=64600000),
    )(block_owner, block_clips, layer_order, *operands)
    hbm = pl.BlockSpec(memory_space=pltpu.HBM)
    scores, peaks = (pltpu.with_memory_space_constraint(a, pltpu.VMEM) for a in (scores, peaks))
    return pl.pallas_call(
        write_out,
        out_shape=(jax.ShapeDtypeStruct(scores.shape, F32), jax.ShapeDtypeStruct(peaks.shape, F32)),
        in_specs=[vmem, vmem],
        out_specs=(hbm, hbm),
        scratch_shapes=[dma((2,))],
        compiler_params=pltpu.CompilerParams(vmem_limit_bytes=1024 * 1024),
    )(scores, peaks)


def solution(mesh):
    in_specs = (
        P(None, ("groups", "tile"), None),
        P("tile", None, None, None),
        P(),
        P(),
        P(("groups", "tile"), None),
    )
    out_specs = (P(None, None, ("groups", "tile"), None), P("groups", None))
    return jax.shard_map(local, mesh=mesh, in_specs=in_specs, out_specs=out_specs, check_vma=False)
```

```python
import functools
import math

import jax
import jax.numpy as jnp
import numpy as np
from jax import lax
from jax.experimental import pallas as pl
from jax.experimental.pallas import tpu as pltpu
from jax.sharding import PartitionSpec as P

F32 = jnp.float32
BF16 = jnp.bfloat16


def split(x):
    high = x.astype(BF16)
    return high, (x - high.astype(F32)).astype(BF16)


def mm(a, b):
    return jnp.dot(a, b, preferred_element_type=F32)


def transform_matrix(extent):
    span = 2 * extent
    odd = 2 * np.arange(extent)[:, None] + 1
    angle = (odd * np.arange(span)[None, :] % (2 * span)) * (math.pi / span)
    return np.concatenate([np.cos(angle), np.sin(angle)], axis=0).astype(np.float32)


def halves(matrix):
    high = matrix.astype(BF16)
    low = (matrix - high.astype(np.float32)).astype(BF16)
    return high, low


def constants(extent):
    forward = transform_matrix(extent)
    fh, fl = halves(forward)
    row_left = np.concatenate([fh, fl, fh], axis=1)
    ft = np.ascontiguousarray(forward.T)
    th, tl = halves(ft)
    col_right = np.stack([th, tl])
    back = forward[:, :extent] * np.float32(1.0 / extent)
    bh, bl = halves(back)
    back_right = np.stack([bh, bl])
    back_left = np.concatenate([bh.T, bl.T, bh.T], axis=1)
    offset = np.arange(2 * extent)[None, :] - np.arange(extent)[:, None]
    band = ((offset >= 0) & (offset < extent)).astype(BF16)
    band_left = np.concatenate([band, band], axis=1)
    band_right = np.ascontiguousarray(band.T)
    return [jnp.asarray(c) for c in (row_left, col_right, back_left, back_right, band_left, band_right)]


def combine(y, e):
    a, b = y[:e, :e], y[:e, e:]
    c, d = y[e:, :e], y[e:, e:]
    return a - d, b + c, a + d, c - b


class Transforms:
    def __init__(self, refs, shapes):
        self.__dict__.update(refs)
        self.layers, self.rows, self.cols, self.e, self.per_block, self.count = shapes
        self.span = 2 * self.e
        self.nc = self.cols // self.e
        self.entries = self.layers * self.e * self.e

    def rows_of(self, b, window):
        e, squares = self.e, None
        for l in range(self.layers):
            x = window(l)
            squares = x * x if squares is None else squares + x * x
            xh, xl = split(x)
            y = mm(self.row_left[...], jnp.concatenate([xh, xh, xl], axis=0))
            h, low = split(y)
            self.yh[l], self.yl[l] = h, low
        sh, sl = split(squares)
        energy = mm(self.band_left[...], jnp.concatenate([sh, sl], axis=0))
        eh, el = split(energy)
        for c in range(self.nc):
            width = min(2, self.nc - c) * e
            at = slice(c * e, c * e + width)
            total = mm(eh[:, at], self.band_right[:width]) + mm(el[:, at], self.band_right[:width])
            self.inv[b, :, c * e:(c + 1) * e] = 1.0 / jnp.sqrt(total / self.entries + 1e-05)

    def columns_of(self, b):
        e = self.e
        for c in range(self.nc):
            width = min(2, self.nc - c) * e
            at = slice(c * e, c * e + width)
            for l in range(self.layers):
                h, low = self.yh[l, :, at], self.yl[l, :, at]
                y = mm(h, self.col_right[0, :width]) + mm(low, self.col_right[0, :width]) + mm(h, self.col_right[1, :width])
                for n, part in enumerate(combine(y, e)):
                    self.tile_parts[b, c, l, n] = part

    def clip_of(self, k, layer_at):
        e, span, row_left, col_right = self.e, self.span, self.row_left, self.col_right
        total = jnp.zeros((e, e), F32)
        for l in range(self.layers):
            chosen = layer_at(l)
            total = total + chosen * chosen
            ch, cl = split(chosen)
            first = mm(row_left[:, :e], ch) + mm(row_left[:, span:span + e], ch) + mm(row_left[:, :e], cl)
            fh, fl = split(first)
            second = mm(fh, col_right[0, :e]) + mm(fl, col_right[0, :e]) + mm(fh, col_right[1, :e])
            for n, part in enumerate(combine(second, e)):
                self.spectra[k, l, n] = part
        mean = jnp.sum(total, keepdims=True) / self.entries
        return 1.0 / (math.sqrt(self.entries) * jnp.sqrt(mean + 1e-05))

    def inverse_of(self, b, k, clip_scale):
        e = self.e
        for c in range(self.nc):
            u1 = u2 = v1 = v2 = None
            for l in range(self.layers):
                p1, p2, q1, q2 = (self.tile_parts[b, c, l, n] for n in range(4))
                c1, c2, d1, d2 = (self.spectra[k, self.order[0, l], n] for n in range(4))
                t = (p1 * c1 + p2 * c2, p2 * c1 - p1 * c2, q1 * d1 + q2 * d2, q2 * d1 - q1 * d2)
                if u1 is None:
                    u1, u2, v1, v2 = t
                else:
                    u1, u2, v1, v2 = u1 + t[0], u2 + t[1], v1 + t[2], v2 + t[3]
            z = jnp.concatenate([
                jnp.concatenate([u1 + v1, u2 - v2], axis=1),
                jnp.concatenate([u2 + v2, v1 - u1], axis=1)], axis=0)
            zh, zl = split(z)
            w = mm(zh, self.back_right[0]) + mm(zl, self.back_right[0]) + mm(zh, self.back_right[1])
            h, low = split(w)
            self.wh[k, :, c * e:(c + 1) * e] = h
            self.wl[k, :, c * e:(c + 1) * e] = low
        out = mm(self.back_left[...], jnp.concatenate([self.wh[k], self.wh[k], self.wl[k]], axis=0))
        out = out * self.inv[b] * (clip_scale * 0.5)
        self.scores[k // self.per_block, k % self.per_block, pl.ds(pl.multiple_of(b * e, e), e)] = out
        top = jnp.max(out, axis=0, keepdims=True)
        best = self.peaks[k:k + 1]
        for c in range(self.nc):
            best = jnp.maximum(best, top[:, c * e:(c + 1) * e])
        self.peaks[k:k + 1] = best


MESH = pl.DeviceIdType.MESH
PLANE = 4
HUBS = 2 * PLANE
CHUNKS = 4


def kernel(tiles_n, owner, picks, order, *refs):
    sources = refs[:8]
    (scores, peak_out,
           yh, yl, inv, tile_parts, spectra, wh, wl, peaks, slots,
           stage, land, full, halo_in,
           rs_send, rs_recv, ag_send, near_recv, far_recv, pair_send, pair_recv,
           halo_send, halo_recv, peak_send, peak_recv,
           library, tiles, row_left, col_right, back_left, back_right, band_left, band_right, load_sem) = refs[8:]
    loads = [pltpu.make_async_copy(a, b, load_sem.at[n]) for n, (a, b) in enumerate(zip(
        sources, (library, tiles, row_left, col_right, back_left, back_right, band_left, band_right)))]
    for load in loads:
        load.start()
    g = lax.axis_index("groups")
    t = lax.axis_index("tile")
    per_block = picks.shape[1]
    layers, rows, cols = tiles.shape
    e = library.shape[-1]
    nr = rows // e
    count = picks.shape[0] * per_block
    work = Transforms(dict(row_left=row_left, col_right=col_right, back_left=back_left, back_right=back_right,
                           band_left=band_left, band_right=band_right, scores=scores, yh=yh, yl=yl, inv=inv,
                           tile_parts=tile_parts, spectra=spectra, wh=wh, wl=wl, peaks=peaks, order=order),
                      (layers, rows, cols, e, per_block, count))
    parity = lax.rem(g, 2)
    other_g = g + 1 - 2 * parity
    core = lax.rem(t, 2)
    partner = (g, t + 1 - 2 * core)
    first_hub = (tiles_n // PLANE // 2 - 1) * PLANE
    is_hub = jnp.logical_and(t >= first_hub, t < first_hub + HUBS)
    others = [(g, lax.rem(t + d, tiles_n)) for d in range(1, tiles_n)]

    barrier = pltpu.get_barrier_semaphore()

    def greet(target):
        pl.semaphore_signal(barrier, inc=1, device_id=target, device_id_type=MESH)

    @pl.when(is_hub)
    def _():
        for target in others:
            greet(target)

    for n in range(HUBS // 2):
        greet((other_g, first_hub + 2 * n + core))

    lanes = count * layers // 2
    width = lanes // CHUNKS
    part = e // HUBS
    loads[0].wait()
    for j in range(lanes):
        slab = 2 * j + parity
        clip, layer = slab // layers, lax.rem(slab, layers)
        block, which = clip // per_block, lax.rem(clip, per_block)
        mask = jnp.where(owner[block] == t, 1.0, 0.0).astype(F32)
        stage[j] = library[picks[block, which], layer] * mask

    pl.semaphore_wait(barrier, jnp.where(is_hub, HUBS - 1 + tiles_n // 2, HUBS))

    def remote(src, dst, send, recv, target):
        return pltpu.make_async_remote_copy(src_ref=src, dst_ref=dst, send_sem=send, recv_sem=recv,
                                            device_id=target, device_id_type=MESH)

    def place(hub):
        at = lax.rem(hub, 2) * (HUBS // 2) + hub // 2
        return pl.ds(pl.multiple_of(at * part, part), part)

    def lane(m):
        return pl.ds(m * width, width)

    mine = pl.ds(pl.multiple_of(core * (e // 2), e // 2), e // 2)
    for m in range(CHUNKS):
        for n in range(HUBS):
            hub = lax.rem(t + n, HUBS)
            target = first_hub + hub
            slot = lax.rem(t - target + tiles_n, tiles_n) - 1

            @pl.when(t != target)
            def _(m=m, hub=hub, target=target, slot=slot):
                remote(stage.at[lane(m), place(hub)], land.at[slot, lane(m)],
                       rs_send.at[m], rs_recv.at[m], (g, target)).start()

    @pl.when(t == tiles_n - 1)
    def _():
        halo_in[...] = jnp.zeros_like(halo_in)

    peaks[...] = jnp.full(peaks.shape, -jnp.inf, F32)
    for load in loads[1:]:
        load.wait()
    for b in range(nr - 1):
        work.rows_of(b, lambda l: tiles[l, b * e:(b + 2) * e])
        work.columns_of(b)

    @pl.when(is_hub)
    def _():
        at = place(t - first_hub)
        for m in range(CHUNKS):
            remote(land.at[:, lane(m)], land.at[:, lane(m)], rs_send.at[m], rs_recv.at[m], partner).wait_recv()
            total = stage[lane(m), at]
            for d in range(tiles_n - 1):
                total = total + land[d, lane(m)]
            full[parity, lane(m), at] = total
            piece = full.at[parity, lane(m), at]
            for n in range(1, tiles_n // 2):
                remote(piece, piece, ag_send.at[m], near_recv.at[m], (g, lax.rem(t + 2 * n, tiles_n))).start()
            for n in range(tiles_n // 2):
                remote(piece, piece, ag_send.at[m], far_recv.at[m], (other_g, lax.rem(t + 2 * n, tiles_n))).start()

    halo = remote(tiles.at[:, pl.ds(0, e)], halo_in, halo_send, halo_recv, (g, t - 1))
    pairs = [remote(full.at[:, lane(m), mine], full.at[:, lane(m), mine], pair_send.at[m], pair_recv.at[m], partner)
             for m in range(CHUNKS)]

    def arrive(m):
        far = full.at[0, lane(m), mine]
        remote(far, far, ag_send.at[m], far_recv.at[m], partner).wait_recv()

        @pl.when(is_hub)
        def _():
            near = full.at[0, lane(m), pl.ds(0, e // 2 - part)]
            remote(near, near, ag_send.at[m], near_recv.at[m], partner).wait_recv()

        @pl.when(jnp.logical_not(is_hub))
        def _():
            remote(far, far, ag_send.at[m], near_recv.at[m], partner).wait_recv()

        pairs[m].start()

    scale = {}

    def clips_in(m):
        slabs = range(2 * m * width, 2 * (m + 1) * width)
        return [k for k in range(count) if (k + 1) * layers - 1 in slabs]

    def slab_of(k, l):
        return full[(k * layers + l) % 2, (k * layers + l) // 2]

    for m in range(CHUNKS + 1):
        if m < CHUNKS:
            arrive(m)
        if m == 0:
            @pl.when(t > 0)
            def _():
                halo.start()
        else:
            pairs[m - 1].wait_recv()
            for k in clips_in(m - 1):
                scale[k] = work.clip_of(k, lambda l: slab_of(k, l))
                for b in range(nr - 1):
                    work.inverse_of(b, k, scale[k])

    @pl.when(t < tiles_n - 1)
    def _():
        halo.wait_recv()
    work.rows_of(nr - 1, lambda l: jnp.concatenate([tiles[l, rows - e:], halo_in[l]], axis=0))
    work.columns_of(nr - 1)
    for k in range(count):
        work.inverse_of(nr - 1, k, scale[k])

    copies = [remote(peaks, slots.at[n], peak_send, peak_recv, target) for n, target in enumerate(others)]
    for copy in copies:
        copy.start()
    for m in range(CHUNKS):
        pairs[m].wait_send()

        @pl.when(is_hub)
        def _(m=m):
            sent = stage.at[lane(m), pl.ds(0, e - part)]
            remote(sent, sent, rs_send.at[m], rs_recv.at[m], partner).wait_send()
            remote(land.at[:, lane(m)], land.at[:, lane(m)], ag_send.at[m], near_recv.at[m], partner).wait_send()

        @pl.when(jnp.logical_not(is_hub))
        def _(m=m):
            sent = stage.at[lane(m)]
            remote(sent, sent, rs_send.at[m], rs_recv.at[m], partner).wait_send()

    @pl.when(t > 0)
    def _():
        halo.wait_send()

    best = peaks[...]
    remote(slots, slots, peak_send, peak_recv, partner).wait_recv()
    for n in range(tiles_n - 1):
        best = jnp.maximum(best, slots[n])
    best = jnp.max(best, axis=1, keepdims=True)
    for k in range(count):
        at = k % per_block
        peak_out[k // per_block:k // per_block + 1, at:at + 1] = best[k:k + 1]
    remote(slots, slots, peak_send, peak_recv, partner).wait_send()


def write_out(scores, peaks, scores_out, peaks_out, sem):
    copies = [pltpu.make_async_copy(scores, scores_out, sem.at[0]), pltpu.make_async_copy(peaks, peaks_out, sem.at[1])]
    for copy in copies:
        copy.start()
    for copy in copies:
        copy.wait()


def local(tiles, library, block_owner, block_clips, layer_order):
    layers, rows, cols = tiles.shape
    e = library.shape[-1]
    span, nr, nc = 2 * e, rows // e, cols // e
    blocks, per_block = block_clips.shape
    count = blocks * per_block
    slabs = count * layers
    lanes = slabs // 2
    assert slabs % 2 == 0 and lanes % CHUNKS == 0
    tiles_n = lax.axis_size("tile")
    smem = pl.BlockSpec(memory_space=pltpu.SMEM)
    vmem = pl.BlockSpec(memory_space=pltpu.VMEM)
    dma = pltpu.SemaphoreType.DMA
    lines = -(-count // 8) * 8
    operands = [library, tiles, *constants(e)]
    scores, peaks = pl.pallas_call(
        functools.partial(kernel, tiles_n),
        out_shape=(pltpu.VMEM((blocks, per_block, rows, cols), F32),
                   pltpu.VMEM((blocks, per_block), F32)),
        in_specs=[smem] * 3 + [pl.BlockSpec(memory_space=pltpu.HBM)] * 8,
        out_specs=(vmem, vmem),
        scratch_shapes=[
            pltpu.VMEM((layers, span, cols), BF16), pltpu.VMEM((layers, span, cols), BF16),
            pltpu.VMEM((nr, e, cols), F32),
            pltpu.VMEM((nr, nc, layers, 4, e, e), F32), pltpu.VMEM((count, layers, 4, e, e), F32),
            pltpu.VMEM((count, span, cols), BF16), pltpu.VMEM((count, span, cols), BF16),
            pltpu.VMEM((lines, e), F32), pltpu.VMEM((tiles_n - 1, lines, e), F32),
            pltpu.VMEM((lanes, e, e), F32), pltpu.VMEM((tiles_n - 1, lanes, e // HUBS, e), F32),
            pltpu.VMEM((2, lanes, e, e), F32), pltpu.VMEM((layers, e, cols), F32),
            *[dma((CHUNKS,))] * 7, dma, dma, dma, dma,
        ] + [pltpu.VMEM(a.shape, a.dtype) for a in operands] + [dma((len(operands),))],
        compiler_params=pltpu.CompilerParams(collective_id=0, has_side_effects=True, vmem_limit_bytes=64600000),
    )(block_owner, block_clips, layer_order, *operands)
    hbm = pl.BlockSpec(memory_space=pltpu.HBM)
    scores, peaks = (pltpu.with_memory_space_constraint(a, pltpu.VMEM) for a in (scores, peaks))
    return pl.pallas_call(
        write_out,
        out_shape=(jax.ShapeDtypeStruct(scores.shape, F32), jax.ShapeDtypeStruct(peaks.shape, F32)),
        in_specs=[vmem, vmem],
        out_specs=(hbm, hbm),
        scratch_shapes=[dma((2,))],
        compiler_params=pltpu.CompilerParams(vmem_limit_bytes=1024 * 1024),
    )(scores, peaks)


def solution(mesh):
    in_specs = (
        P(None, ("groups", "tile"), None),
        P("tile", None, None, None),
        P(),
        P(),
        P(("groups", "tile"), None),
    )
    out_specs = (P(None, None, ("groups", "tile"), None), P("groups", None))
    return jax.shard_map(local, mesh=mesh, in_specs=in_specs, out_specs=out_specs, check_vma=False)
```

```python
import functools
import math

import jax
import jax.numpy as jnp
import numpy as np
from jax import lax
from jax.experimental import pallas as pl
from jax.experimental.pallas import tpu as pltpu
from jax.sharding import PartitionSpec as P

F32 = jnp.float32
BF16 = jnp.bfloat16


def split(x):
    high = x.astype(BF16)
    return high, (x - high.astype(F32)).astype(BF16)


def mm(a, b):
    return jnp.dot(a, b, preferred_element_type=F32)


def transform_matrix(extent):
    span = 2 * extent
    odd = 2 * np.arange(extent)[:, None] + 1
    angle = (odd * np.arange(span)[None, :] % (2 * span)) * (math.pi / span)
    return np.concatenate([np.cos(angle), np.sin(angle)], axis=0).astype(np.float32)


def cyclic_matrix(extent):
    span = 2 * extent
    angle = (np.arange(extent)[:, None] * np.arange(span)[None, :] % span) * (2 * math.pi / span)
    cosine, sine = np.cos(angle), np.sin(angle)
    sine[0] = 1 - 2 * (np.arange(span) % 2)
    return np.concatenate([cosine, sine], axis=0).astype(np.float32)


def halves(matrix):
    high = matrix.astype(BF16)
    low = (matrix - high.astype(np.float32)).astype(BF16)
    return high, low


def constants(extent):
    forward = transform_matrix(extent)
    rings = [cyclic_matrix(extent), forward]
    fh, fl = halves(forward)
    row_left = np.concatenate([fh, fl, fh], axis=1)
    col_right = np.stack([np.stack(halves(np.ascontiguousarray(r.T))) for r in rings])
    bh, bl = halves(np.ascontiguousarray(forward[:, :extent].T) * np.float32(1.0 / extent))
    back_left = np.concatenate([bh, bh, bl], axis=1)
    back_right = np.stack([np.stack(halves(r * np.float32(0.5 / extent))) for r in rings])
    offset = np.arange(2 * extent)[None, :] - np.arange(extent)[:, None]
    band = ((offset >= 0) & (offset < extent)).astype(BF16)
    band_left = np.concatenate([band, band], axis=1)
    band_right = np.ascontiguousarray(band.T)
    return [jnp.asarray(c) for c in (row_left, col_right, back_left, back_right, band_left, band_right)]


class Transforms:
    def __init__(self, refs, shapes):
        self.__dict__.update(refs)
        self.layers, self.rows, self.cols, self.e, self.per_block, self.count = shapes
        self.span = 2 * self.e
        self.nc = self.cols // self.e
        self.entries = self.layers * self.e * self.e

    def special(self):
        return lax.broadcasted_iota(jnp.int32, (self.e, self.e), 1) == 0

    def combine(self, y, cyclic):
        e = self.e
        a, b = y[:e, :e], y[:e, e:]
        c, d = y[e:, :e], y[e:, e:]
        parts = a - d, b + c, a + d, c - b
        if cyclic:
            first = self.special()
            parts = [jnp.where(first, own, part) for own, part in zip((a, c, b, d), parts)]
        return parts

    def weights(self, matrix, ring, rows):
        return jnp.concatenate([matrix[ring, 0, :rows], matrix[ring, 0, :rows], matrix[ring, 1, :rows]], axis=0)

    def tile_of(self, b, window):
        e, squares = self.e, None
        for l in range(self.layers):
            x = window(l)
            squares = x * x if squares is None else squares + x * x
            xh, xl = split(x)
            y = mm(self.row_left[...], jnp.concatenate([xh, xh, xl], axis=0))
            head, middle, tail = y[:, :e], y[:, e:2 * e], y[:, 2 * e:]
            mh, ml = split(middle)
            for ring, start in enumerate((head + tail, head - tail)):
                sh, sl = split(start)
                y = mm(jnp.concatenate([sh, mh, sl, ml, sh, mh], axis=1), self.weights(self.col_right, ring, 2 * e))
                for n, part in enumerate(self.combine(y, ring == 0)):
                    self.tile_parts[b, l, ring, n] = part
        sh, sl = split(squares)
        energy = mm(self.band_left[...], jnp.concatenate([sh, sl], axis=0))
        eh, el = split(energy)
        for c in range(self.nc):
            width = min(2, self.nc - c) * e
            at = slice(c * e, c * e + width)
            total = mm(eh[:, at], self.band_right[:width]) + mm(el[:, at], self.band_right[:width])
            self.inv[b, :, c * e:(c + 1) * e] = 1.0 / jnp.sqrt(total / self.entries + 1e-05)

    def clip_of(self, k, layer_at):
        e, span, row_left = self.e, self.span, self.row_left
        chosen = [layer_at(l) for l in range(self.layers)]
        total = sum(x * x for x in chosen)
        ch, cl = split(jnp.concatenate(chosen, axis=1))
        left = jnp.concatenate([row_left[:, n * span:n * span + e] for n in range(3)], axis=1)
        first = mm(left, jnp.concatenate([ch, ch, cl], axis=0))
        fh, fl = split(jnp.concatenate([first[:, l * e:(l + 1) * e] for l in range(self.layers)], axis=0))
        left = jnp.concatenate([fh, fl, fh], axis=1)
        for ring in range(2):
            y = mm(left, self.weights(self.col_right, ring, e))
            for l in range(self.layers):
                for n, part in enumerate(self.combine(y[l * span:(l + 1) * span], ring == 0)):
                    self.spectra[k, l, ring, n] = part
        mean = jnp.sum(total, keepdims=True) / self.entries
        return 1.0 / (math.sqrt(self.entries) * jnp.sqrt(mean + 1e-05))

    def inverse_of(self, b, k, clip_scale):
        e, rings = self.e, []
        for ring in range(2):
            u1 = u2 = v1 = v2 = None
            for l in range(self.layers):
                p1, p2, q1, q2 = (self.tile_parts[b, l, ring, n] for n in range(4))
                c1, c2, d1, d2 = (self.spectra[k, self.order[0, l], ring, n] for n in range(4))
                t = (p1 * c1 + p2 * c2, p2 * c1 - p1 * c2, q1 * d1 + q2 * d2, q2 * d1 - q1 * d2)
                if u1 is None:
                    u1, u2, v1, v2 = t
                else:
                    u1, u2, v1, v2 = u1 + t[0], u2 + t[1], v1 + t[2], v2 + t[3]
            parts = u1 + v1, u2 - v2, u2 + v2, v1 - u1
            if ring == 0:
                first = self.special()
                parts = [jnp.where(first, own, part) for own, part in zip((u1, v1, u2, v2), parts)]
            z = jnp.concatenate([jnp.concatenate(parts[:2], axis=1), jnp.concatenate(parts[2:], axis=1)], axis=0)
            zh, zl = split(z)
            wh, wl = split(mm(self.back_left[...], jnp.concatenate([zh, zl, zh], axis=0)))
            rings.append(mm(jnp.concatenate([wh, wl, wh], axis=1), self.weights(self.back_right, ring, 2 * e)))
        scale = clip_scale * 0.5
        best = self.peaks[k:k + 1]
        for c in range(self.nc):
            n = c % 2
            even, odd = (r[:, n * e:(n + 1) * e] for r in rings)
            out = (even + odd if c < 2 else even - odd) * (self.inv[b, :, c * e:(c + 1) * e] * scale)
            self.scores[k // self.per_block, k % self.per_block, b * e:(b + 1) * e, c * e:(c + 1) * e] = out
            best = jnp.maximum(best, jnp.max(out, axis=0, keepdims=True))
        self.peaks[k:k + 1] = best


MESH = pl.DeviceIdType.MESH
PLANE = 4
HUBS = 2 * PLANE
CHUNKS = 4


def kernel(tiles_n, owner, picks, order, *refs):
    sources = refs[:8]
    (scores, peak_out,
           inv, tile_parts, spectra, peaks, slots,
           stage, land, full, halo_in,
           rs_send, rs_recv, ag_send, near_recv, far_recv, pair_send, pair_recv,
           halo_send, halo_recv, peak_send, peak_recv,
           library, tiles, row_left, col_right, back_left, back_right, band_left, band_right, load_sem) = refs[8:]
    loads = [pltpu.make_async_copy(a, b, load_sem.at[n]) for n, (a, b) in enumerate(zip(
        sources, (library, tiles, row_left, col_right, back_left, back_right, band_left, band_right)))]
    for load in loads:
        load.start()
    g = lax.axis_index("groups")
    t = lax.axis_index("tile")
    per_block = picks.shape[1]
    layers, rows, cols = tiles.shape
    e = library.shape[-1]
    nr = rows // e
    count = picks.shape[0] * per_block
    work = Transforms(dict(row_left=row_left, col_right=col_right, back_left=back_left, back_right=back_right,
                           band_left=band_left, band_right=band_right, scores=scores, inv=inv,
                           tile_parts=tile_parts, spectra=spectra, peaks=peaks, order=order),
                      (layers, rows, cols, e, per_block, count))
    parity = lax.rem(g, 2)
    other_g = g + 1 - 2 * parity
    core = lax.rem(t, 2)
    partner = (g, t + 1 - 2 * core)
    first_hub = (tiles_n // PLANE // 2 - 1) * PLANE
    is_hub = jnp.logical_and(t >= first_hub, t < first_hub + HUBS)
    others = [(g, lax.rem(t + d, tiles_n)) for d in range(1, tiles_n)]

    barrier = pltpu.get_barrier_semaphore()

    def greet(target):
        pl.semaphore_signal(barrier, inc=1, device_id=target, device_id_type=MESH)

    @pl.when(is_hub)
    def _():
        for target in others:
            greet(target)

    for n in range(HUBS // 2):
        greet((other_g, first_hub + 2 * n + core))

    lanes = count * layers // 2
    width = lanes // CHUNKS
    part = e // HUBS
    loads[0].wait()
    for j in range(lanes):
        slab = 2 * j + parity
        clip, layer = slab // layers, lax.rem(slab, layers)
        block, which = clip // per_block, lax.rem(clip, per_block)
        mask = jnp.where(owner[block] == t, 1.0, 0.0).astype(F32)
        stage[j] = library[picks[block, which], layer] * mask

    pl.semaphore_wait(barrier, jnp.where(is_hub, HUBS - 1 + tiles_n // 2, HUBS))

    def remote(src, dst, send, recv, target):
        return pltpu.make_async_remote_copy(src_ref=src, dst_ref=dst, send_sem=send, recv_sem=recv,
                                            device_id=target, device_id_type=MESH)

    def place(hub):
        at = lax.rem(hub, 2) * (HUBS // 2) + hub // 2
        return pl.ds(pl.multiple_of(at * part, part), part)

    def lane(m):
        return pl.ds(m * width, width)

    mine = pl.ds(pl.multiple_of(core * (e // 2), e // 2), e // 2)
    for m in range(CHUNKS):
        for n in range(HUBS):
            hub = lax.rem(t + n, HUBS)
            target = first_hub + hub
            slot = lax.rem(t - target + tiles_n, tiles_n) - 1

            @pl.when(t != target)
            def _(m=m, hub=hub, target=target, slot=slot):
                remote(stage.at[lane(m), place(hub)], land.at[slot, lane(m)],
                       rs_send.at[m], rs_recv.at[m], (g, target)).start()

    @pl.when(t == tiles_n - 1)
    def _():
        halo_in[...] = jnp.zeros_like(halo_in)

    peaks[...] = jnp.full(peaks.shape, -jnp.inf, F32)
    for load in loads[1:]:
        load.wait()
    for b in range(nr - 1):
        work.tile_of(b, lambda l: tiles[l, b * e:(b + 2) * e])

    @pl.when(is_hub)
    def _():
        at = place(t - first_hub)
        for m in range(CHUNKS):
            remote(land.at[:, lane(m)], land.at[:, lane(m)], rs_send.at[m], rs_recv.at[m], partner).wait_recv()
            total = stage[lane(m), at]
            for d in range(tiles_n - 1):
                total = total + land[d, lane(m)]
            full[parity, lane(m), at] = total
            piece = full.at[parity, lane(m), at]
            for n in range(1, tiles_n // 2):
                remote(piece, piece, ag_send.at[m], near_recv.at[m], (g, lax.rem(t + 2 * n, tiles_n))).start()
            for n in range(tiles_n // 2):
                remote(piece, piece, ag_send.at[m], far_recv.at[m], (other_g, lax.rem(t + 2 * n, tiles_n))).start()

    halo = remote(tiles.at[:, pl.ds(0, e)], halo_in, halo_send, halo_recv, (g, t - 1))
    pairs = [remote(full.at[:, lane(m), mine], full.at[:, lane(m), mine], pair_send.at[m], pair_recv.at[m], partner)
             for m in range(CHUNKS)]

    def arrive(m):
        far = full.at[0, lane(m), mine]
        remote(far, far, ag_send.at[m], far_recv.at[m], partner).wait_recv()

        @pl.when(is_hub)
        def _():
            near = full.at[0, lane(m), pl.ds(0, e // 2 - part)]
            remote(near, near, ag_send.at[m], near_recv.at[m], partner).wait_recv()

        @pl.when(jnp.logical_not(is_hub))
        def _():
            remote(far, far, ag_send.at[m], near_recv.at[m], partner).wait_recv()

        pairs[m].start()

    scale = {}

    def clips_in(m):
        slabs = range(2 * m * width, 2 * (m + 1) * width)
        return [k for k in range(count) if (k + 1) * layers - 1 in slabs]

    def slab_of(k, l):
        return full[(k * layers + l) % 2, (k * layers + l) // 2]

    for m in range(CHUNKS + 1):
        if m < CHUNKS:
            arrive(m)
        if m == 0:
            @pl.when(t > 0)
            def _():
                halo.start()
        else:
            pairs[m - 1].wait_recv()
            for k in clips_in(m - 1):
                scale[k] = work.clip_of(k, lambda l: slab_of(k, l))
                for b in range(nr - 1):
                    work.inverse_of(b, k, scale[k])

    @pl.when(t < tiles_n - 1)
    def _():
        halo.wait_recv()
    work.tile_of(nr - 1, lambda l: jnp.concatenate([tiles[l, rows - e:], halo_in[l]], axis=0))
    for k in range(count):
        work.inverse_of(nr - 1, k, scale[k])

    copies = [remote(peaks, slots.at[n], peak_send, peak_recv, target) for n, target in enumerate(others)]
    for copy in copies:
        copy.start()
    for m in range(CHUNKS):
        pairs[m].wait_send()

        @pl.when(is_hub)
        def _(m=m):
            sent = stage.at[lane(m), pl.ds(0, e - part)]
            remote(sent, sent, rs_send.at[m], rs_recv.at[m], partner).wait_send()
            remote(land.at[:, lane(m)], land.at[:, lane(m)], ag_send.at[m], near_recv.at[m], partner).wait_send()

        @pl.when(jnp.logical_not(is_hub))
        def _(m=m):
            sent = stage.at[lane(m)]
            remote(sent, sent, rs_send.at[m], rs_recv.at[m], partner).wait_send()

    @pl.when(t > 0)
    def _():
        halo.wait_send()

    best = peaks[...]
    remote(slots, slots, peak_send, peak_recv, partner).wait_recv()
    for n in range(tiles_n - 1):
        best = jnp.maximum(best, slots[n])
    best = jnp.max(best, axis=1, keepdims=True)
    for k in range(count):
        at = k % per_block
        peak_out[k // per_block:k // per_block + 1, at:at + 1] = best[k:k + 1]
    remote(slots, slots, peak_send, peak_recv, partner).wait_send()


def write_out(scores, peaks, scores_out, peaks_out, sem):
    copies = [pltpu.make_async_copy(scores, scores_out, sem.at[0]), pltpu.make_async_copy(peaks, peaks_out, sem.at[1])]
    for copy in copies:
        copy.start()
    for copy in copies:
        copy.wait()


def local(tiles, library, block_owner, block_clips, layer_order):
    layers, rows, cols = tiles.shape
    e = library.shape[-1]
    nr = rows // e
    assert cols == 3 * e
    blocks, per_block = block_clips.shape
    count = blocks * per_block
    slabs = count * layers
    lanes = slabs // 2
    assert slabs % 2 == 0 and lanes % CHUNKS == 0
    tiles_n = lax.axis_size("tile")
    smem = pl.BlockSpec(memory_space=pltpu.SMEM)
    vmem = pl.BlockSpec(memory_space=pltpu.VMEM)
    dma = pltpu.SemaphoreType.DMA
    lines = -(-count // 8) * 8
    operands = [library, tiles, *constants(e)]
    scores, peaks = pl.pallas_call(
        functools.partial(kernel, tiles_n),
        out_shape=(pltpu.VMEM((blocks, per_block, rows, cols), F32),
                   pltpu.VMEM((blocks, per_block), F32)),
        in_specs=[smem] * 3 + [pl.BlockSpec(memory_space=pltpu.HBM)] * 8,
        out_specs=(vmem, vmem),
        scratch_shapes=[
            pltpu.VMEM((nr, e, cols), F32),
            pltpu.VMEM((nr, layers, 2, 4, e, e), F32), pltpu.VMEM((count, layers, 2, 4, e, e), F32),
            pltpu.VMEM((lines, e), F32), pltpu.VMEM((tiles_n - 1, lines, e), F32),
            pltpu.VMEM((lanes, e, e), F32), pltpu.VMEM((tiles_n - 1, lanes, e // HUBS, e), F32),
            pltpu.VMEM((2, lanes, e, e), F32), pltpu.VMEM((layers, e, cols), F32),
            *[dma((CHUNKS,))] * 7, dma, dma, dma, dma,
        ] + [pltpu.VMEM(a.shape, a.dtype) for a in operands] + [dma((len(operands),))],
        compiler_params=pltpu.CompilerParams(collective_id=0, has_side_effects=True, vmem_limit_bytes=64600000),
    )(block_owner, block_clips, layer_order, *operands)
    hbm = pl.BlockSpec(memory_space=pltpu.HBM)
    scores, peaks = (pltpu.with_memory_space_constraint(a, pltpu.VMEM) for a in (scores, peaks))
    return pl.pallas_call(
        write_out,
        out_shape=(jax.ShapeDtypeStruct(scores.shape, F32), jax.ShapeDtypeStruct(peaks.shape, F32)),
        in_specs=[vmem, vmem],
        out_specs=(hbm, hbm),
        scratch_shapes=[dma((2,))],
        compiler_params=pltpu.CompilerParams(vmem_limit_bytes=1024 * 1024),
    )(scores, peaks)


def solution(mesh):
    in_specs = (
        P(None, ("groups", "tile"), None),
        P("tile", None, None, None),
        P(),
        P(),
        P(("groups", "tile"), None),
    )
    out_specs = (P(None, None, ("groups", "tile"), None), P("groups", None))
    return jax.shard_map(local, mesh=mesh, in_specs=in_specs, out_specs=out_specs, check_vma=False)
```

```python
import functools
import math

import jax
import jax.numpy as jnp
import numpy as np
from jax import lax
from jax.experimental import pallas as pl
from jax.experimental.pallas import tpu as pltpu
from jax.sharding import PartitionSpec as P

F32 = jnp.float32
BF16 = jnp.bfloat16


def split(x):
    high = x.astype(BF16)
    return high, (x - high.astype(F32)).astype(BF16)


def mm(a, b):
    return jnp.dot(a, b, preferred_element_type=F32)


def transform_matrix(extent):
    span = 2 * extent
    odd = 2 * np.arange(extent)[:, None] + 1
    angle = (odd * np.arange(span)[None, :] % (2 * span)) * (math.pi / span)
    return np.concatenate([np.cos(angle), np.sin(angle)], axis=0).astype(np.float32)


def cyclic_matrix(extent):
    span = 2 * extent
    angle = (np.arange(extent)[:, None] * np.arange(span)[None, :] % span) * (2 * math.pi / span)
    cosine, sine = np.cos(angle), np.sin(angle)
    sine[0] = 1 - 2 * (np.arange(span) % 2)
    return np.concatenate([cosine, sine], axis=0).astype(np.float32)


def halves(matrix):
    high = matrix.astype(BF16)
    low = (matrix - high.astype(np.float32)).astype(BF16)
    return high, low


def constants(extent):
    forward = transform_matrix(extent)
    rings = [cyclic_matrix(extent), forward]
    fh, fl = halves(forward)
    row_left = np.concatenate([fh, fl, fh], axis=1)
    col_right = np.stack([np.stack(halves(np.ascontiguousarray(r.T))) for r in rings])
    bh, bl = halves(np.ascontiguousarray(forward[:, :extent].T) * np.float32(1.0 / extent))
    back_left = np.concatenate([bh, bh, bl], axis=1)
    back_right = np.stack([np.stack(halves(r * np.float32(0.5 / extent))) for r in rings])
    offset = np.arange(2 * extent)[None, :] - np.arange(extent)[:, None]
    band = ((offset >= 0) & (offset < extent)).astype(BF16)
    band_left = np.concatenate([band, band], axis=1)
    band_right = np.ascontiguousarray(band.T)
    return [jnp.asarray(c) for c in (row_left, col_right, back_left, back_right, band_left, band_right)]


class Transforms:
    def __init__(self, refs, shapes):
        self.__dict__.update(refs)
        self.layers, self.rows, self.cols, self.e, self.per_block, self.count = shapes
        self.span = 2 * self.e
        self.nc = self.cols // self.e
        self.entries = self.layers * self.e * self.e

    def special(self):
        return lax.broadcasted_iota(jnp.int32, (self.e, self.e), 1) == 0

    def combine(self, y, cyclic):
        e = self.e
        a, b = y[:e, :e], y[:e, e:]
        c, d = y[e:, :e], y[e:, e:]
        parts = a - d, b + c, a + d, c - b
        if cyclic:
            first = self.special()
            parts = [jnp.where(first, own, part) for own, part in zip((a, c, b, d), parts)]
        return parts

    def weights(self, matrix, ring, rows):
        return jnp.concatenate([matrix[ring, 0, :rows], matrix[ring, 0, :rows], matrix[ring, 1, :rows]], axis=0)

    def tile_of(self, b, window):
        e, squares = self.e, None
        for l in range(self.layers):
            x = window(self.layer_of[l])
            squares = x * x if squares is None else squares + x * x
            xh, xl = split(x)
            y = mm(self.row_left[...], jnp.concatenate([xh, xh, xl], axis=0))
            head, middle, tail = y[:, :e], y[:, e:2 * e], y[:, 2 * e:]
            mh, ml = split(middle)
            for ring, start in enumerate((head + tail, head - tail)):
                sh, sl = split(start)
                y = mm(jnp.concatenate([sh, mh, sl, ml, sh, mh], axis=1), self.weights(self.col_right, ring, 2 * e))
                for n, part in enumerate(self.combine(y, ring == 0)):
                    self.tile_parts[b, l, ring, n] = part
        sh, sl = split(squares)
        energy = mm(self.band_left[...], jnp.concatenate([sh, sl], axis=0))
        eh, el = split(energy)
        for c in range(self.nc):
            width = min(2, self.nc - c) * e
            at = slice(c * e, c * e + width)
            total = mm(eh[:, at], self.band_right[:width]) + mm(el[:, at], self.band_right[:width])
            self.inv[b, :, c * e:(c + 1) * e] = 1.0 / jnp.sqrt(total / self.entries + 1e-05)

    def clip_of(self, k, layer_at):
        e, span, row_left = self.e, self.span, self.row_left
        chosen = [layer_at(l) for l in range(self.layers)]
        total = sum(x * x for x in chosen)
        ch, cl = split(jnp.concatenate(chosen, axis=1))
        left = jnp.concatenate([row_left[:, n * span:n * span + e] for n in range(3)], axis=1)
        first = mm(left, jnp.concatenate([ch, ch, cl], axis=0))
        fh, fl = split(jnp.concatenate([first[:, l * e:(l + 1) * e] for l in range(self.layers)], axis=0))
        left = jnp.concatenate([fh, fl, fh], axis=1)
        for ring in range(2):
            y = mm(left, self.weights(self.col_right, ring, e))
            for l in range(self.layers):
                for n, part in enumerate(self.combine(y[l * span:(l + 1) * span], ring == 0)):
                    self.spectra[k, l, ring, n] = part
        mean = jnp.sum(total, keepdims=True) / self.entries
        self.scale[k] = jnp.broadcast_to(0.5 / (math.sqrt(self.entries) * jnp.sqrt(mean + 1e-05)), (1, e))

    def product_of(self, b, k, ring):
        u1 = u2 = v1 = v2 = None
        for l in range(self.layers):
            p1, p2, q1, q2 = (self.tile_parts[b, l, ring, n] for n in range(4))
            c1, c2, d1, d2 = (self.spectra[k, l, ring, n] for n in range(4))
            t = (p1 * c1 + p2 * c2, p2 * c1 - p1 * c2, q1 * d1 + q2 * d2, q2 * d1 - q1 * d2)
            if u1 is None:
                u1, u2, v1, v2 = t
            else:
                u1, u2, v1, v2 = u1 + t[0], u2 + t[1], v1 + t[2], v2 + t[3]
        parts = u1 + v1, u2 - v2, u2 + v2, v1 - u1
        if ring == 0:
            first = self.special()
            parts = [jnp.where(first, own, part) for own, part in zip((u1, v1, u2, v2), parts)]
        return jnp.concatenate([jnp.concatenate(parts[:2], axis=1), jnp.concatenate(parts[2:], axis=1)], axis=0)

    def rows_of(self, z):
        e, span, left = self.e, self.span, self.back_left
        zh, zl = split(z)
        both = mm(jnp.concatenate([left[:, :span], left[:, 2 * span:]], axis=0), zh)
        return both[:e] + both[e:] + mm(left[:, :span], zl)

    def inverse_of(self, items):
        e, rings = self.e, []
        for ring in range(2):
            wh, wl = zip(*(split(self.rows_of(self.product_of(b, k, ring))) for b, k in items))
            wh, wl = jnp.concatenate(wh, axis=0), jnp.concatenate(wl, axis=0)
            both = mm(jnp.concatenate([wh, wl], axis=0), self.back_right[ring, 0])
            rings.append(both[:len(items) * e] + both[len(items) * e:] + mm(wh, self.back_right[ring, 1]))
        for n, (b, k) in enumerate(items):
            scale = self.scale[k]
            best = self.peaks[k]
            for c in range(self.nc):
                even, odd = (r[n * e:(n + 1) * e, c % 2 * e:(c % 2 + 1) * e] for r in rings)
                out = (even + odd if c < 2 else even - odd) * (self.inv[b, :, c * e:(c + 1) * e] * scale)
                at = pl.ds(pl.multiple_of(b * e, e), e)
                self.scores[k // self.per_block, lax.rem(k, self.per_block), at, c * e:(c + 1) * e] = out
                best = jnp.maximum(best, jnp.max(out, axis=0, keepdims=True))
            self.peaks[k] = best


MESH = pl.DeviceIdType.MESH
PLANE = 4
HUBS = 2 * PLANE
UNROLL = 4


def kernel(tiles_n, owner, picks, order, *refs):
    sources = refs[:8]
    (scores, peak_out,
           inv, tile_parts, spectra, scale, peaks, best, slots,
           stage, land, full, halo_in,
           rs_send, rs_recv, ag_send, near_recv, far_recv, pair_send, pair_recv,
           halo_send, halo_recv, peak_send, peak_recv,
           library, tiles, row_left, col_right, back_left, back_right, band_left, band_right, load_sem) = refs[8:]
    loads = [pltpu.make_async_copy(a, b, load_sem.at[n]) for n, (a, b) in enumerate(zip(
        sources, (library, tiles, row_left, col_right, back_left, back_right, band_left, band_right)))]
    for load in loads:
        load.start()
    g = lax.axis_index("groups")
    t = lax.axis_index("tile")
    per_block = picks.shape[1]
    layers, rows, cols = tiles.shape
    e = library.shape[-1]
    nr = rows // e
    count = picks.shape[0] * per_block
    layer_of = [sum(jnp.where(order[0, l] == own, l, 0) for l in range(1, layers)) for own in range(layers)]
    work = Transforms(dict(row_left=row_left, col_right=col_right, back_left=back_left, back_right=back_right,
                           band_left=band_left, band_right=band_right, scores=scores, inv=inv,
                           tile_parts=tile_parts, spectra=spectra, scale=scale, peaks=best, layer_of=layer_of),
                      (layers, rows, cols, e, per_block, count))
    parity = lax.rem(g, 2)
    other_g = g + 1 - 2 * parity
    core = lax.rem(t, 2)
    partner = (g, t + 1 - 2 * core)
    first_hub = (tiles_n // PLANE // 2 - 1) * PLANE
    is_hub = jnp.logical_and(t >= first_hub, t < first_hub + HUBS)
    others = [(g, lax.rem(t + d, tiles_n)) for d in range(1, tiles_n)]

    barrier = pltpu.get_barrier_semaphore()

    def greet(target):
        pl.semaphore_signal(barrier, inc=1, device_id=target, device_id_type=MESH)

    @pl.when(is_hub)
    def _():
        for target in others:
            greet(target)

    for n in range(HUBS // 2):
        greet((other_g, first_hub + 2 * n + core))

    lanes = count * layers // 2
    width = lanes // count
    part = e // HUBS
    loads[0].wait()
    for j in range(lanes):
        slab = 2 * j + parity
        clip, layer = slab // layers, lax.rem(slab, layers)
        block, which = clip // per_block, lax.rem(clip, per_block)
        mask = jnp.where(owner[block] == t, 1.0, 0.0).astype(F32)
        stage[j] = library[picks[block, which], layer] * mask

    pl.semaphore_wait(barrier, jnp.where(is_hub, HUBS - 1 + tiles_n // 2, HUBS))

    def remote(src, dst, send, recv, target):
        return pltpu.make_async_remote_copy(src_ref=src, dst_ref=dst, send_sem=send, recv_sem=recv,
                                            device_id=target, device_id_type=MESH)

    def place(hub):
        at = lax.rem(hub, 2) * (HUBS // 2) + hub // 2
        return pl.ds(pl.multiple_of(at * part, part), part)

    def lane(m):
        return pl.ds(m * width, width)

    mine = pl.ds(pl.multiple_of(core * (e // 2), e // 2), e // 2)
    for m in range(count):
        for n in range(HUBS):
            hub = lax.rem(t + n, HUBS)
            target = first_hub + hub
            slot = lax.rem(t - target + tiles_n, tiles_n) - 1

            @pl.when(t != target)
            def _(m=m, hub=hub, target=target, slot=slot):
                remote(stage.at[lane(m), place(hub)], land.at[slot, lane(m)],
                       rs_send.at[m], rs_recv.at[m], (g, target)).start()

    @pl.when(t == tiles_n - 1)
    def _():
        halo_in[...] = jnp.zeros_like(halo_in)

    peaks[...] = jnp.full(peaks.shape, -jnp.inf, F32)
    best[...] = jnp.full(best.shape, -jnp.inf, F32)
    for load in loads[1:]:
        load.wait()
    def tile_block(b, carry):
        work.tile_of(b, lambda l: tiles[l, pl.ds(pl.multiple_of(b * e, e), 2 * e)])
        return carry

    lax.fori_loop(0, nr - 1, tile_block, 0)

    @pl.when(is_hub)
    def _():
        at = place(t - first_hub)
        for m in range(count):
            remote(land.at[:, lane(m)], land.at[:, lane(m)], rs_send.at[m], rs_recv.at[m], partner).wait_recv()
            total = stage[lane(m), at]
            for d in range(tiles_n - 1):
                total = total + land[d, lane(m)]
            full[parity, lane(m), at] = total
            piece = full.at[parity, lane(m), at]
            for n in range(1, tiles_n // 2):
                remote(piece, piece, ag_send.at[m], near_recv.at[m], (g, lax.rem(t + 2 * n, tiles_n))).start()
            for n in range(tiles_n // 2):
                remote(piece, piece, ag_send.at[m], far_recv.at[m], (other_g, lax.rem(t + 2 * n, tiles_n))).start()

    halo = remote(tiles.at[:, pl.ds(0, e)], halo_in, halo_send, halo_recv, (g, t - 1))
    def pair(m):
        return remote(full.at[:, lane(m), mine], full.at[:, lane(m), mine], pair_send.at[m], pair_recv.at[m], partner)

    def arrive(m):
        far = full.at[0, lane(m), mine]
        remote(far, far, ag_send.at[m], far_recv.at[m], partner).wait_recv()

        @pl.when(is_hub)
        def _():
            near = full.at[0, lane(m), pl.ds(0, e // 2 - part)]
            remote(near, near, ag_send.at[m], near_recv.at[m], partner).wait_recv()

        @pl.when(jnp.logical_not(is_hub))
        def _():
            remote(far, far, ag_send.at[m], near_recv.at[m], partner).wait_recv()

        pair(m).start()

    arrive(0)

    @pl.when(t > 0)
    def _():
        halo.start()

    def clip_block(k, carry):
        @pl.when(k < count - 1)
        def _():
            arrive(k + 1)

        pair(k).wait_recv()
        work.clip_of(k, lambda l: full[l, k])
        for b in range(nr - 1):
            work.inverse_of([(b, k)])
        return carry

    lax.fori_loop(0, count, clip_block, 0)

    @pl.when(t < tiles_n - 1)
    def _():
        halo.wait_recv()
    work.tile_of(nr - 1, lambda l: jnp.concatenate([tiles[l, rows - e:], halo_in[l]], axis=0))

    def last_block(k, carry):
        for n in range(UNROLL):
            work.inverse_of([(nr - 1, UNROLL * k + n)])
        return carry

    lax.fori_loop(0, count // UNROLL, last_block, 0)
    for k in range(count):
        peaks[k:k + 1] = best[k]

    copies = [remote(peaks, slots.at[n], peak_send, peak_recv, target) for n, target in enumerate(others)]
    for copy in copies:
        copy.start()
    for m in range(count):
        pair(m).wait_send()

        @pl.when(is_hub)
        def _(m=m):
            sent = stage.at[lane(m), pl.ds(0, e - part)]
            remote(sent, sent, rs_send.at[m], rs_recv.at[m], partner).wait_send()
            remote(land.at[:, lane(m)], land.at[:, lane(m)], ag_send.at[m], near_recv.at[m], partner).wait_send()

        @pl.when(jnp.logical_not(is_hub))
        def _(m=m):
            sent = stage.at[lane(m)]
            remote(sent, sent, rs_send.at[m], rs_recv.at[m], partner).wait_send()

    @pl.when(t > 0)
    def _():
        halo.wait_send()

    top = peaks[...]
    remote(slots, slots, peak_send, peak_recv, partner).wait_recv()
    for n in range(tiles_n - 1):
        top = jnp.maximum(top, slots[n])
    top = jnp.max(top, axis=1, keepdims=True)
    for k in range(count):
        at = k % per_block
        peak_out[k // per_block:k // per_block + 1, at:at + 1] = top[k:k + 1]
    remote(slots, slots, peak_send, peak_recv, partner).wait_send()


def write_out(scores, peaks, scores_out, peaks_out, sem):
    copies = [pltpu.make_async_copy(scores, scores_out, sem.at[0]), pltpu.make_async_copy(peaks, peaks_out, sem.at[1])]
    for copy in copies:
        copy.start()
    for copy in copies:
        copy.wait()


def local(tiles, library, block_owner, block_clips, layer_order):
    layers, rows, cols = tiles.shape
    e = library.shape[-1]
    nr = rows // e
    assert cols == 3 * e
    blocks, per_block = block_clips.shape
    count = blocks * per_block
    slabs = count * layers
    lanes = slabs // 2
    assert layers == 2 and count % UNROLL == 0
    tiles_n = lax.axis_size("tile")
    smem = pl.BlockSpec(memory_space=pltpu.SMEM)
    vmem = pl.BlockSpec(memory_space=pltpu.VMEM)
    dma = pltpu.SemaphoreType.DMA
    lines = -(-count // 8) * 8
    operands = [library, tiles, *constants(e)]
    scores, peaks = pl.pallas_call(
        functools.partial(kernel, tiles_n),
        out_shape=(pltpu.VMEM((blocks, per_block, rows, cols), F32),
                   pltpu.VMEM((blocks, per_block), F32)),
        in_specs=[smem] * 3 + [pl.BlockSpec(memory_space=pltpu.HBM)] * 8,
        out_specs=(vmem, vmem),
        scratch_shapes=[
            pltpu.VMEM((nr, e, cols), F32),
            pltpu.VMEM((nr, layers, 2, 4, e, e), F32), pltpu.VMEM((count, layers, 2, 4, e, e), F32),
            pltpu.VMEM((count, 1, e), F32), pltpu.VMEM((lines, e), F32), pltpu.VMEM((count, 1, e), F32),
            pltpu.VMEM((tiles_n - 1, lines, e), F32),
            pltpu.VMEM((lanes, e, e), F32), pltpu.VMEM((tiles_n - 1, lanes, e // HUBS, e), F32),
            pltpu.VMEM((2, lanes, e, e), F32), pltpu.VMEM((layers, e, cols), F32),
            *[dma((count,))] * 7, dma, dma, dma, dma,
        ] + [pltpu.VMEM(a.shape, a.dtype) for a in operands] + [dma((len(operands),))],
        compiler_params=pltpu.CompilerParams(collective_id=0, has_side_effects=True, vmem_limit_bytes=64600000),
    )(block_owner, block_clips, layer_order, *operands)
    hbm = pl.BlockSpec(memory_space=pltpu.HBM)
    scores, peaks = (pltpu.with_memory_space_constraint(a, pltpu.VMEM) for a in (scores, peaks))
    return pl.pallas_call(
        write_out,
        out_shape=(jax.ShapeDtypeStruct(scores.shape, F32), jax.ShapeDtypeStruct(peaks.shape, F32)),
        in_specs=[vmem, vmem],
        out_specs=(hbm, hbm),
        scratch_shapes=[dma((2,))],
        compiler_params=pltpu.CompilerParams(vmem_limit_bytes=1024 * 1024),
    )(scores, peaks)


def solution(mesh):
    in_specs = (
        P(None, ("groups", "tile"), None),
        P("tile", None, None, None),
        P(),
        P(),
        P(("groups", "tile"), None),
    )
    out_specs = (P(None, None, ("groups", "tile"), None), P("groups", None))
    return jax.shard_map(local, mesh=mesh, in_specs=in_specs, out_specs=out_specs, check_vma=False)
```

```python
import functools
import math

import jax
import jax.numpy as jnp
import numpy as np
from jax import lax
from jax.experimental import pallas as pl
from jax.experimental.pallas import tpu as pltpu
from jax.sharding import PartitionSpec as P

F32 = jnp.float32
BF16 = jnp.bfloat16


def split(x):
    high = x.astype(BF16)
    return high, (x - high.astype(F32)).astype(BF16)


def mm(a, b):
    return jnp.dot(a, b, preferred_element_type=F32)


def transform_matrix(extent):
    span = 2 * extent
    odd = 2 * np.arange(extent)[:, None] + 1
    angle = (odd * np.arange(span)[None, :] % (2 * span)) * (math.pi / span)
    return np.concatenate([np.cos(angle), np.sin(angle)], axis=0).astype(np.float32)


def cyclic_matrix(extent):
    span = 2 * extent
    angle = (np.arange(extent)[:, None] * np.arange(span)[None, :] % span) * (2 * math.pi / span)
    cosine, sine = np.cos(angle), np.sin(angle)
    sine[0] = 1 - 2 * (np.arange(span) % 2)
    return np.concatenate([cosine, sine], axis=0).astype(np.float32)


def halves(matrix):
    high = matrix.astype(BF16)
    low = (matrix - high.astype(np.float32)).astype(BF16)
    return high, low


def constants(extent):
    forward = transform_matrix(extent)
    rings = [cyclic_matrix(extent), forward]
    fh, fl = halves(forward)
    row_left = np.concatenate([fh, fl, fh], axis=1)
    col_right = np.stack([np.stack(halves(np.ascontiguousarray(r.T))) for r in rings])
    bh, bl = halves(np.ascontiguousarray(forward[:, :extent].T) * np.float32(1.0 / extent))
    back_left = np.concatenate([bh, bh, bl], axis=1)
    back_right = np.stack([np.stack(halves(r * np.float32(0.5 / extent))) for r in rings])
    offset = np.arange(2 * extent)[None, :] - np.arange(extent)[:, None]
    band = ((offset >= 0) & (offset < extent)).astype(BF16)
    band_left = np.concatenate([band, band], axis=1)
    band_right = np.ascontiguousarray(band.T)
    return [jnp.asarray(c) for c in (row_left, col_right, back_left, back_right, band_left, band_right)]


class Transforms:
    def __init__(self, refs, shapes):
        self.__dict__.update(refs)
        self.layers, self.rows, self.cols, self.e, self.per_block, self.count = shapes
        self.span = 2 * self.e
        self.nc = self.cols // self.e
        self.entries = self.layers * self.e * self.e

    def special(self):
        return lax.broadcasted_iota(jnp.int32, (self.e, self.e), 1) == 0

    def combine(self, y, cyclic):
        e = self.e
        a, b = y[:e, :e], y[:e, e:]
        c, d = y[e:, :e], y[e:, e:]
        parts = a - d, b + c, a + d, c - b
        if cyclic:
            first = self.special()
            parts = [jnp.where(first, own, part) for own, part in zip((a, c, b, d), parts)]
        return parts

    def weights(self, matrix, ring, rows):
        return jnp.concatenate([matrix[ring, 0, :rows], matrix[ring, 0, :rows], matrix[ring, 1, :rows]], axis=0)

    def tile_of(self, b, window):
        e, squares = self.e, None
        for l in range(self.layers):
            x = window(self.layer_of[l])
            squares = x * x if squares is None else squares + x * x
            xh, xl = split(x)
            y = mm(self.row_left[...], jnp.concatenate([xh, xh, xl], axis=0))
            head, middle, tail = y[:, :e], y[:, e:2 * e], y[:, 2 * e:]
            mh, ml = split(middle)
            for ring, start in enumerate((head + tail, head - tail)):
                sh, sl = split(start)
                y = mm(jnp.concatenate([sh, mh, sl, ml, sh, mh], axis=1), self.weights(self.col_right, ring, 2 * e))
                for n, part in enumerate(self.combine(y, ring == 0)):
                    self.tile_parts[b, l, ring, n] = part
        sh, sl = split(squares)
        energy = mm(self.band_left[...], jnp.concatenate([sh, sl], axis=0))
        eh, el = split(energy)
        for c in range(self.nc):
            width = min(2, self.nc - c) * e
            at = slice(c * e, c * e + width)
            total = mm(eh[:, at], self.band_right[:width]) + mm(el[:, at], self.band_right[:width])
            self.inv[b, :, c * e:(c + 1) * e] = 1.0 / jnp.sqrt(total / self.entries + 1e-05)

    def clip_of(self, k, layer_at):
        e, span, row_left = self.e, self.span, self.row_left
        chosen = [layer_at(l) for l in range(self.layers)]
        total = sum(x * x for x in chosen)
        ch, cl = split(jnp.concatenate(chosen, axis=1))
        left = jnp.concatenate([row_left[:, n * span:n * span + e] for n in range(3)], axis=1)
        first = mm(left, jnp.concatenate([ch, ch, cl], axis=0))
        fh, fl = split(jnp.concatenate([first[:, l * e:(l + 1) * e] for l in range(self.layers)], axis=0))
        left = jnp.concatenate([fh, fl, fh], axis=1)
        for ring in range(2):
            y = mm(left, self.weights(self.col_right, ring, e))
            for l in range(self.layers):
                for n, part in enumerate(self.combine(y[l * span:(l + 1) * span], ring == 0)):
                    self.spectra[k, l, ring, n] = part
        mean = jnp.sum(total, keepdims=True) / self.entries
        self.scale[k] = jnp.broadcast_to(0.5 / (math.sqrt(self.entries) * jnp.sqrt(mean + 1e-05)), (1, e))

    def product_of(self, b, k, ring):
        u1 = u2 = v1 = v2 = None
        for l in range(self.layers):
            p1, p2, q1, q2 = (self.tile_parts[b, l, ring, n] for n in range(4))
            c1, c2, d1, d2 = (self.spectra[k, l, ring, n] for n in range(4))
            t = (p1 * c1 + p2 * c2, p2 * c1 - p1 * c2, q1 * d1 + q2 * d2, q2 * d1 - q1 * d2)
            if u1 is None:
                u1, u2, v1, v2 = t
            else:
                u1, u2, v1, v2 = u1 + t[0], u2 + t[1], v1 + t[2], v2 + t[3]
        parts = u1 + v1, u2 - v2, u2 + v2, v1 - u1
        if ring == 0:
            first = self.special()
            parts = [jnp.where(first, own, part) for own, part in zip((u1, v1, u2, v2), parts)]
        return jnp.concatenate([jnp.concatenate(parts[:2], axis=1), jnp.concatenate(parts[2:], axis=1)], axis=0)

    def rows_of(self, z):
        e, span, left = self.e, self.span, self.back_left
        zh, zl = split(z)
        both = mm(jnp.concatenate([left[:, :span], left[:, 2 * span:]], axis=0), zh)
        return both[:e] + both[e:] + mm(left[:, :span], zl)

    def inverse_of(self, items):
        e, rings = self.e, []
        for ring in range(2):
            wh, wl = zip(*(split(self.rows_of(self.product_of(b, k, ring))) for b, k in items))
            wh, wl = jnp.concatenate(wh, axis=0), jnp.concatenate(wl, axis=0)
            both = mm(jnp.concatenate([wh, wl], axis=0), self.back_right[ring, 0])
            rings.append(both[:len(items) * e] + both[len(items) * e:] + mm(wh, self.back_right[ring, 1]))
        for n, (b, k) in enumerate(items):
            scale = self.scale[k]
            best = self.peaks[k]
            for c in range(self.nc):
                even, odd = (r[n * e:(n + 1) * e, c % 2 * e:(c % 2 + 1) * e] for r in rings)
                out = (even + odd if c < 2 else even - odd) * (self.inv[b, :, c * e:(c + 1) * e] * scale)
                at = pl.ds(pl.multiple_of(b * e, e), e)
                self.scores[k // self.per_block, k % self.per_block, at, c * e:(c + 1) * e] = out
                best = jnp.maximum(best, jnp.max(out, axis=0, keepdims=True))
            self.peaks[k] = best


MESH = pl.DeviceIdType.MESH
PLANE = 4
HUBS = 2 * PLANE
UNROLL = 4


def kernel(tiles_n, owner, picks, order, *refs):
    sources = refs[:8]
    (scores, peak_out,
           inv, tile_parts, spectra, scale, peaks, best, slots,
           stage, land, full, halo_in,
           rs_send, rs_recv, ag_send, near_recv, far_recv, pair_send, pair_recv,
           halo_send, halo_recv, peak_send, peak_recv,
           library, tiles, row_left, col_right, back_left, back_right, band_left, band_right, load_sem) = refs[8:]
    loads = [pltpu.make_async_copy(a, b, load_sem.at[n]) for n, (a, b) in enumerate(zip(
        sources, (library, tiles, row_left, col_right, back_left, back_right, band_left, band_right)))]
    for load in loads:
        load.start()
    g = lax.axis_index("groups")
    t = lax.axis_index("tile")
    per_block = picks.shape[1]
    layers, rows, cols = tiles.shape
    e = library.shape[-1]
    nr = rows // e
    count = picks.shape[0] * per_block
    layer_of = [sum(jnp.where(order[0, l] == own, l, 0) for l in range(1, layers)) for own in range(layers)]
    work = Transforms(dict(row_left=row_left, col_right=col_right, back_left=back_left, back_right=back_right,
                           band_left=band_left, band_right=band_right, scores=scores, inv=inv,
                           tile_parts=tile_parts, spectra=spectra, scale=scale, peaks=best, layer_of=layer_of),
                      (layers, rows, cols, e, per_block, count))
    parity = lax.rem(g, 2)
    other_g = g + 1 - 2 * parity
    core = lax.rem(t, 2)
    partner = (g, t + 1 - 2 * core)
    first_hub = (tiles_n // PLANE // 2 - 1) * PLANE
    is_hub = jnp.logical_and(t >= first_hub, t < first_hub + HUBS)
    others = [(g, lax.rem(t + d, tiles_n)) for d in range(1, tiles_n)]

    barrier = pltpu.get_barrier_semaphore()

    def greet(target):
        pl.semaphore_signal(barrier, inc=1, device_id=target, device_id_type=MESH)

    @pl.when(is_hub)
    def _():
        for target in others:
            greet(target)

    for n in range(HUBS // 2):
        greet((other_g, first_hub + 2 * n + core))

    lanes = count * layers // 2
    width = lanes // count
    part = e // HUBS
    loads[0].wait()
    for j in range(lanes):
        slab = 2 * j + parity
        clip, layer = slab // layers, lax.rem(slab, layers)
        block, which = clip // per_block, lax.rem(clip, per_block)
        mask = jnp.where(owner[block] == t, 1.0, 0.0).astype(F32)
        stage[j] = library[picks[block, which], layer] * mask

    pl.semaphore_wait(barrier, jnp.where(is_hub, HUBS - 1 + tiles_n // 2, HUBS))

    def remote(src, dst, send, recv, target):
        return pltpu.make_async_remote_copy(src_ref=src, dst_ref=dst, send_sem=send, recv_sem=recv,
                                            device_id=target, device_id_type=MESH)

    def place(hub):
        at = lax.rem(hub, 2) * (HUBS // 2) + hub // 2
        return pl.ds(pl.multiple_of(at * part, part), part)

    def lane(m):
        return pl.ds(m * width, width)

    mine = pl.ds(pl.multiple_of(core * (e // 2), e // 2), e // 2)
    for m in range(count):
        for n in range(HUBS):
            hub = lax.rem(t + n, HUBS)
            target = first_hub + hub
            slot = lax.rem(t - target + tiles_n, tiles_n) - 1

            @pl.when(t != target)
            def _(m=m, hub=hub, target=target, slot=slot):
                remote(stage.at[lane(m), place(hub)], land.at[slot, lane(m)],
                       rs_send.at[m], rs_recv.at[m], (g, target)).start()

    @pl.when(t == tiles_n - 1)
    def _():
        halo_in[...] = jnp.zeros_like(halo_in)

    peaks[...] = jnp.full(peaks.shape, -jnp.inf, F32)
    best[...] = jnp.full(best.shape, -jnp.inf, F32)
    for load in loads[1:]:
        load.wait()
    def tile_block(b, carry):
        work.tile_of(b, lambda l: tiles[l, pl.ds(pl.multiple_of(b * e, e), 2 * e)])
        return carry

    lax.fori_loop(0, nr - 1, tile_block, 0)

    @pl.when(is_hub)
    def _():
        at = place(t - first_hub)
        for m in range(count):
            remote(land.at[:, lane(m)], land.at[:, lane(m)], rs_send.at[m], rs_recv.at[m], partner).wait_recv()
            total = stage[lane(m), at]
            for d in range(tiles_n - 1):
                total = total + land[d, lane(m)]
            full[parity, lane(m), at] = total
            piece = full.at[parity, lane(m), at]
            for n in range(1, tiles_n // 2):
                remote(piece, piece, ag_send.at[m], near_recv.at[m], (g, lax.rem(t + 2 * n, tiles_n))).start()
            for n in range(tiles_n // 2):
                remote(piece, piece, ag_send.at[m], far_recv.at[m], (other_g, lax.rem(t + 2 * n, tiles_n))).start()

    halo = remote(tiles.at[:, pl.ds(0, e)], halo_in, halo_send, halo_recv, (g, t - 1))
    def pair(m):
        return remote(full.at[:, lane(m), mine], full.at[:, lane(m), mine], pair_send.at[m], pair_recv.at[m], partner)

    def arrive(m):
        far = full.at[0, lane(m), mine]
        remote(far, far, ag_send.at[m], far_recv.at[m], partner).wait_recv()

        @pl.when(is_hub)
        def _():
            near = full.at[0, lane(m), pl.ds(0, e // 2 - part)]
            remote(near, near, ag_send.at[m], near_recv.at[m], partner).wait_recv()

        @pl.when(jnp.logical_not(is_hub))
        def _():
            remote(far, far, ag_send.at[m], near_recv.at[m], partner).wait_recv()

        pair(m).start()

    arrive(0)

    @pl.when(t > 0)
    def _():
        halo.start()

    for k in range(count):
        if k < count - 1:
            arrive(k + 1)
        pair(k).wait_recv()
        for b in range(nr - 1 if k else 0):
            work.inverse_of([(b, k - 1)])
        work.clip_of(k, lambda l: full[l, k])

    @pl.when(t < tiles_n - 1)
    def _():
        halo.wait_recv()
    work.tile_of(nr - 1, lambda l: jnp.concatenate([tiles[l, rows - e:], halo_in[l]], axis=0))
    for b in range(nr - 1):
        work.inverse_of([(b, count - 1)])
    for k in range(count):
        work.inverse_of([(nr - 1, k)])
    for k in range(count):
        peaks[k:k + 1] = best[k]

    copies = [remote(peaks, slots.at[n], peak_send, peak_recv, target) for n, target in enumerate(others)]
    for copy in copies:
        copy.start()
    for m in range(count):
        pair(m).wait_send()

        @pl.when(is_hub)
        def _(m=m):
            sent = stage.at[lane(m), pl.ds(0, e - part)]
            remote(sent, sent, rs_send.at[m], rs_recv.at[m], partner).wait_send()
            remote(land.at[:, lane(m)], land.at[:, lane(m)], ag_send.at[m], near_recv.at[m], partner).wait_send()

        @pl.when(jnp.logical_not(is_hub))
        def _(m=m):
            sent = stage.at[lane(m)]
            remote(sent, sent, rs_send.at[m], rs_recv.at[m], partner).wait_send()

    @pl.when(t > 0)
    def _():
        halo.wait_send()

    top = peaks[...]
    remote(slots, slots, peak_send, peak_recv, partner).wait_recv()
    for n in range(tiles_n - 1):
        top = jnp.maximum(top, slots[n])
    top = jnp.max(top, axis=1, keepdims=True)
    for k in range(count):
        at = k % per_block
        peak_out[k // per_block:k // per_block + 1, at:at + 1] = top[k:k + 1]
    remote(slots, slots, peak_send, peak_recv, partner).wait_send()


def write_out(scores, peaks, scores_out, peaks_out, sem):
    copies = [pltpu.make_async_copy(scores, scores_out, sem.at[0]), pltpu.make_async_copy(peaks, peaks_out, sem.at[1])]
    for copy in copies:
        copy.start()
    for copy in copies:
        copy.wait()


def local(tiles, library, block_owner, block_clips, layer_order):
    layers, rows, cols = tiles.shape
    e = library.shape[-1]
    nr = rows // e
    assert cols == 3 * e
    blocks, per_block = block_clips.shape
    count = blocks * per_block
    slabs = count * layers
    lanes = slabs // 2
    assert layers == 2 and count % UNROLL == 0
    tiles_n = lax.axis_size("tile")
    smem = pl.BlockSpec(memory_space=pltpu.SMEM)
    vmem = pl.BlockSpec(memory_space=pltpu.VMEM)
    dma = pltpu.SemaphoreType.DMA
    lines = -(-count // 8) * 8
    operands = [library, tiles, *constants(e)]
    scores, peaks = pl.pallas_call(
        functools.partial(kernel, tiles_n),
        out_shape=(pltpu.VMEM((blocks, per_block, rows, cols), F32),
                   pltpu.VMEM((blocks, per_block), F32)),
        in_specs=[smem] * 3 + [pl.BlockSpec(memory_space=pltpu.HBM)] * 8,
        out_specs=(vmem, vmem),
        scratch_shapes=[
            pltpu.VMEM((nr, e, cols), F32),
            pltpu.VMEM((nr, layers, 2, 4, e, e), F32), pltpu.VMEM((count, layers, 2, 4, e, e), F32),
            pltpu.VMEM((count, 1, e), F32), pltpu.VMEM((lines, e), F32), pltpu.VMEM((count, 1, e), F32),
            pltpu.VMEM((tiles_n - 1, lines, e), F32),
            pltpu.VMEM((lanes, e, e), F32), pltpu.VMEM((tiles_n - 1, lanes, e // HUBS, e), F32),
            pltpu.VMEM((2, lanes, e, e), F32), pltpu.VMEM((layers, e, cols), F32),
            *[dma((count,))] * 7, dma, dma, dma, dma,
        ] + [pltpu.VMEM(a.shape, a.dtype) for a in operands] + [dma((len(operands),))],
        compiler_params=pltpu.CompilerParams(collective_id=0, has_side_effects=True, vmem_limit_bytes=64600000),
    )(block_owner, block_clips, layer_order, *operands)
    hbm = pl.BlockSpec(memory_space=pltpu.HBM)
    scores, peaks = (pltpu.with_memory_space_constraint(a, pltpu.VMEM) for a in (scores, peaks))
    return pl.pallas_call(
        write_out,
        out_shape=(jax.ShapeDtypeStruct(scores.shape, F32), jax.ShapeDtypeStruct(peaks.shape, F32)),
        in_specs=[vmem, vmem],
        out_specs=(hbm, hbm),
        scratch_shapes=[dma((2,))],
        compiler_params=pltpu.CompilerParams(vmem_limit_bytes=1024 * 1024),
    )(scores, peaks)


def solution(mesh):
    in_specs = (
        P(None, ("groups", "tile"), None),
        P("tile", None, None, None),
        P(),
        P(),
        P(("groups", "tile"), None),
    )
    out_specs = (P(None, None, ("groups", "tile"), None), P("groups", None))
    return jax.shard_map(local, mesh=mesh, in_specs=in_specs, out_specs=out_specs, check_vma=False)
```

```python
import functools
import math

import jax
import jax.numpy as jnp
import numpy as np
from jax import lax
from jax.experimental import pallas as pl
from jax.experimental.pallas import tpu as pltpu
from jax.sharding import PartitionSpec as P

F32 = jnp.float32
BF16 = jnp.bfloat16


def split(x):
    high = x.astype(BF16)
    return high, (x - high.astype(F32)).astype(BF16)


def mm(a, b):
    return jnp.dot(a, b, preferred_element_type=F32)


def transform_matrix(extent):
    span = 2 * extent
    odd = 2 * np.arange(extent)[:, None] + 1
    angle = (odd * np.arange(span)[None, :] % (2 * span)) * (math.pi / span)
    return np.concatenate([np.cos(angle), np.sin(angle)], axis=0).astype(np.float32)


def cyclic_matrix(extent):
    span = 2 * extent
    angle = (np.arange(extent)[:, None] * np.arange(span)[None, :] % span) * (2 * math.pi / span)
    cosine, sine = np.cos(angle), np.sin(angle)
    sine[0] = 1 - 2 * (np.arange(span) % 2)
    return np.concatenate([cosine, sine], axis=0).astype(np.float32)


def halves(matrix):
    high = matrix.astype(BF16)
    low = (matrix - high.astype(np.float32)).astype(BF16)
    return high, low


def constants(extent):
    forward = transform_matrix(extent)
    rings = [cyclic_matrix(extent), forward]
    fh, fl = halves(forward)
    row_left = np.concatenate([fh, fl, fh], axis=1)
    col_right = np.stack([np.stack(halves(np.ascontiguousarray(r.T))) for r in rings])
    bh, bl = halves(np.ascontiguousarray(forward[:, :extent].T) * np.float32(1.0 / extent))
    back_left = np.concatenate([bh, bh, bl], axis=1)
    back_right = np.stack([np.stack(halves(r * np.float32(0.5 / extent))) for r in rings])
    offset = np.arange(2 * extent)[None, :] - np.arange(extent)[:, None]
    band = ((offset >= 0) & (offset < extent)).astype(BF16)
    band_left = np.concatenate([band, band], axis=1)
    band_right = np.ascontiguousarray(band.T)
    return [jnp.asarray(c) for c in (row_left, col_right, back_left, back_right, band_left, band_right)]


class Transforms:
    def __init__(self, refs, shapes):
        self.__dict__.update(refs)
        self.layers, self.rows, self.cols, self.e, self.per_block, self.count = shapes
        self.span = 2 * self.e
        self.nc = self.cols // self.e
        self.entries = self.layers * self.e * self.e

    def special(self):
        return lax.broadcasted_iota(jnp.int32, (self.e, self.e), 1) == 0

    def combine(self, y, cyclic):
        e = self.e
        a, b = y[:e, :e], y[:e, e:]
        c, d = y[e:, :e], y[e:, e:]
        parts = a - d, b + c, a + d, c - b
        if cyclic:
            first = self.special()
            parts = [jnp.where(first, own, part) for own, part in zip((a, c, b, d), parts)]
        return parts

    def weights(self, matrix, ring, rows):
        return jnp.concatenate([matrix[ring, 0, :rows], matrix[ring, 0, :rows], matrix[ring, 1, :rows]], axis=0)

    def tile_of(self, b, window):
        e, squares = self.e, None
        for l in range(self.layers):
            x = window(self.layer_of[l])
            squares = x * x if squares is None else squares + x * x
            xh, xl = split(x)
            y = mm(self.row_left[...], jnp.concatenate([xh, xh, xl], axis=0))
            head, middle, tail = y[:, :e], y[:, e:2 * e], y[:, 2 * e:]
            mh, ml = split(middle)
            for ring, start in enumerate((head + tail, head - tail)):
                sh, sl = split(start)
                y = mm(jnp.concatenate([sh, mh, sl, ml, sh, mh], axis=1), self.weights(self.col_right, ring, 2 * e))
                for n, part in enumerate(self.combine(y, ring == 0)):
                    self.tile_parts[b, l, ring, n] = part
        sh, sl = split(squares)
        energy = mm(self.band_left[...], jnp.concatenate([sh, sl], axis=0))
        eh, el = split(energy)
        for c in range(self.nc):
            width = min(2, self.nc - c) * e
            at = slice(c * e, c * e + width)
            total = mm(eh[:, at], self.band_right[:width]) + mm(el[:, at], self.band_right[:width])
            self.inv[b, :, c * e:(c + 1) * e] = 1.0 / jnp.sqrt(total / self.entries + 1e-05)

    def clip_of(self, k, layer_at):
        e, span, row_left = self.e, self.span, self.row_left
        chosen = [layer_at(l) for l in range(self.layers)]
        total = sum(x * x for x in chosen)
        ch, cl = split(jnp.concatenate(chosen, axis=1))
        left = jnp.concatenate([row_left[:, n * span:n * span + e] for n in range(3)], axis=1)
        first = mm(left, jnp.concatenate([ch, ch, cl], axis=0))
        fh, fl = split(jnp.concatenate([first[:, l * e:(l + 1) * e] for l in range(self.layers)], axis=0))
        left = jnp.concatenate([fh, fl, fh], axis=1)
        for ring in range(2):
            y = mm(left, self.weights(self.col_right, ring, e))
            for l in range(self.layers):
                for n, part in enumerate(self.combine(y[l * span:(l + 1) * span], ring == 0)):
                    self.spectra[k, l, ring, n] = part
        mean = jnp.sum(total, keepdims=True) / self.entries
        self.scale[k] = jnp.broadcast_to(0.5 / (math.sqrt(self.entries) * jnp.sqrt(mean + 1e-05)), (1, e))

    def product_of(self, b, k, ring):
        u1 = u2 = v1 = v2 = None
        for l in range(self.layers):
            p1, p2, q1, q2 = (self.tile_parts[b, l, ring, n] for n in range(4))
            c1, c2, d1, d2 = (self.spectra[k, l, ring, n] for n in range(4))
            t = (p1 * c1 + p2 * c2, p2 * c1 - p1 * c2, q1 * d1 + q2 * d2, q2 * d1 - q1 * d2)
            if u1 is None:
                u1, u2, v1, v2 = t
            else:
                u1, u2, v1, v2 = u1 + t[0], u2 + t[1], v1 + t[2], v2 + t[3]
        parts = u1 + v1, u2 - v2, u2 + v2, v1 - u1
        if ring == 0:
            first = self.special()
            parts = [jnp.where(first, own, part) for own, part in zip((u1, v1, u2, v2), parts)]
        return jnp.concatenate([jnp.concatenate(parts[:2], axis=1), jnp.concatenate(parts[2:], axis=1)], axis=0)

    def rows_of(self, z):
        e, span, left = self.e, self.span, self.back_left
        zh, zl = split(z)
        both = mm(jnp.concatenate([left[:, :span], left[:, 2 * span:]], axis=0), zh)
        return both[:e] + both[e:] + mm(left[:, :span], zl)

    def inverse_of(self, items):
        e, rings = self.e, []
        for ring in range(2):
            wh, wl = zip(*(split(self.rows_of(self.product_of(b, k, ring))) for b, k in items))
            wh, wl = jnp.concatenate(wh, axis=0), jnp.concatenate(wl, axis=0)
            both = mm(jnp.concatenate([wh, wl], axis=0), self.back_right[ring, 0])
            rings.append(both[:len(items) * e] + both[len(items) * e:] + mm(wh, self.back_right[ring, 1]))
        for n, (b, k) in enumerate(items):
            scale = self.scale[k]
            best = self.peaks[k]
            for c in range(self.nc):
                even, odd = (r[n * e:(n + 1) * e, c % 2 * e:(c % 2 + 1) * e] for r in rings)
                out = (even + odd if c < 2 else even - odd) * (self.inv[b, :, c * e:(c + 1) * e] * scale)
                at = pl.ds(pl.multiple_of(b * e, e), e)
                self.scores[k // self.per_block, k % self.per_block, at, c * e:(c + 1) * e] = out
                best = jnp.maximum(best, jnp.max(out, axis=0, keepdims=True))
            self.peaks[k] = best


MESH = pl.DeviceIdType.MESH
PLANE = 4
HUBS = 2 * PLANE
UNROLL = 4


def kernel(tiles_n, owner, picks, order, *refs):
    sources = refs[:8]
    (scores, peak_out,
           inv, tile_parts, spectra, scale, peaks, best, slots,
           stage, land, full, halo_in,
           rs_send, rs_recv, ag_send, near_recv, far_recv, pair_send, pair_recv,
           halo_send, halo_recv, peak_send, peak_recv,
           library, tiles, row_left, col_right, back_left, back_right, band_left, band_right, load_sem) = refs[8:]
    loads = [pltpu.make_async_copy(a, b, load_sem.at[n]) for n, (a, b) in enumerate(zip(
        sources, (library, tiles, row_left, col_right, back_left, back_right, band_left, band_right)))]
    for load in loads:
        load.start()
    g = lax.axis_index("groups")
    t = lax.axis_index("tile")
    per_block = picks.shape[1]
    layers, rows, cols = tiles.shape
    e = library.shape[-1]
    nr = rows // e
    count = picks.shape[0] * per_block
    layer_of = [sum(jnp.where(order[0, l] == own, l, 0) for l in range(1, layers)) for own in range(layers)]
    work = Transforms(dict(row_left=row_left, col_right=col_right, back_left=back_left, back_right=back_right,
                           band_left=band_left, band_right=band_right, scores=scores, inv=inv,
                           tile_parts=tile_parts, spectra=spectra, scale=scale, peaks=best, layer_of=layer_of),
                      (layers, rows, cols, e, per_block, count))
    parity = lax.rem(g, 2)
    other_g = g + 1 - 2 * parity
    core = lax.rem(t, 2)
    partner = (g, t + 1 - 2 * core)
    first_hub = (tiles_n // PLANE // 2 - 1) * PLANE
    is_hub = jnp.logical_and(t >= first_hub, t < first_hub + HUBS)
    others = [(g, lax.rem(t + d, tiles_n)) for d in range(1, tiles_n)]

    barrier = pltpu.get_barrier_semaphore()

    def greet(target):
        pl.semaphore_signal(barrier, inc=1, device_id=target, device_id_type=MESH)

    @pl.when(is_hub)
    def _():
        for target in others:
            greet(target)

    for n in range(HUBS // 2):
        greet((other_g, first_hub + 2 * n + core))

    lanes = count * layers // 2
    width = lanes // count
    part = e // HUBS
    loads[0].wait()
    for j in range(lanes):
        slab = 2 * j + parity
        clip, layer = slab // layers, lax.rem(slab, layers)
        block, which = clip // per_block, lax.rem(clip, per_block)
        mask = jnp.where(owner[block] == t, 1.0, 0.0).astype(F32)
        stage[j] = library[picks[block, which], layer] * mask

    pl.semaphore_wait(barrier, jnp.where(is_hub, HUBS - 1 + tiles_n // 2, HUBS))

    def remote(src, dst, send, recv, target):
        return pltpu.make_async_remote_copy(src_ref=src, dst_ref=dst, send_sem=send, recv_sem=recv,
                                            device_id=target, device_id_type=MESH)

    def place(hub):
        at = lax.rem(hub, 2) * (HUBS // 2) + hub // 2
        return pl.ds(pl.multiple_of(at * part, part), part)

    def lane(m):
        return pl.ds(m * width, width)

    mine = pl.ds(pl.multiple_of(core * (e // 2), e // 2), e // 2)
    for m in range(count):
        for n in range(HUBS):
            hub = lax.rem(t + n, HUBS)
            target = first_hub + hub
            slot = lax.rem(t - target + tiles_n, tiles_n) - 1

            @pl.when(t != target)
            def _(m=m, hub=hub, target=target, slot=slot):
                remote(stage.at[lane(m), place(hub)], land.at[slot, lane(m)],
                       rs_send.at[m], rs_recv.at[m], (g, target)).start()

    @pl.when(t == tiles_n - 1)
    def _():
        halo_in[...] = jnp.zeros_like(halo_in)

    peaks[...] = jnp.full(peaks.shape, -jnp.inf, F32)
    best[...] = jnp.full(best.shape, -jnp.inf, F32)
    for load in loads[1:]:
        load.wait()
    def tile_block(b, carry):
        work.tile_of(b, lambda l: tiles[l, pl.ds(pl.multiple_of(b * e, e), 2 * e)])
        return carry

    lax.fori_loop(0, nr - 1, tile_block, 0)

    @pl.when(is_hub)
    def _():
        at = place(t - first_hub)
        for m in range(count):
            remote(land.at[:, lane(m)], land.at[:, lane(m)], rs_send.at[m], rs_recv.at[m], partner).wait_recv()
            total = stage[lane(m), at]
            for d in range(tiles_n - 1):
                total = total + land[d, lane(m)]
            full[parity, lane(m), at] = total
            piece = full.at[parity, lane(m), at]
            for n in range(1, tiles_n // 2):
                remote(piece, piece, ag_send.at[m], near_recv.at[m], (g, lax.rem(t + 2 * n, tiles_n))).start()
            for n in range(tiles_n // 2):
                remote(piece, piece, ag_send.at[m], far_recv.at[m], (other_g, lax.rem(t + 2 * n, tiles_n))).start()

    halo = remote(tiles.at[:, pl.ds(0, e)], halo_in, halo_send, halo_recv, (g, t - 1))
    def pair(m):
        return remote(full.at[:, lane(m), mine], full.at[:, lane(m), mine], pair_send.at[m], pair_recv.at[m], partner)

    def arrive(m):
        far = full.at[0, lane(m), mine]
        remote(far, far, ag_send.at[m], far_recv.at[m], partner).wait_recv()

        @pl.when(is_hub)
        def _():
            near = full.at[0, lane(m), pl.ds(0, e // 2 - part)]
            remote(near, near, ag_send.at[m], near_recv.at[m], partner).wait_recv()

        @pl.when(jnp.logical_not(is_hub))
        def _():
            remote(far, far, ag_send.at[m], near_recv.at[m], partner).wait_recv()

        pair(m).start()

    arrive(0)

    @pl.when(t > 0)
    def _():
        halo.start()

    for k in range(count):
        if k < count - 1:
            arrive(k + 1)
        pair(k).wait_recv()
        for b in range(nr - 1 if k else 0):
            work.inverse_of([(b, k - 1)])
        work.clip_of(k, lambda l: full[l, k])

    @pl.when(t < tiles_n - 1)
    def _():
        halo.wait_recv()
    work.tile_of(nr - 1, lambda l: jnp.concatenate([tiles[l, rows - e:], halo_in[l]], axis=0))
    for b in range(nr - 1):
        work.inverse_of([(b, count - 1)])
    for k in range(count):
        work.inverse_of([(nr - 1, k)])
    for k in range(count):
        peaks[k:k + 1] = best[k]

    for n in range(tiles_n):
        target = jnp.where(t < tiles_n // 2, tiles_n - 1 - n, n)

        @pl.when(target != t)
        def _(target=target):
            slot = lax.rem(t - target + tiles_n, tiles_n) - 1
            remote(peaks, slots.at[slot], peak_send, peak_recv, (g, target)).start()
    for m in range(count):
        pair(m).wait_send()

        @pl.when(is_hub)
        def _(m=m):
            sent = stage.at[lane(m), pl.ds(0, e - part)]
            remote(sent, sent, rs_send.at[m], rs_recv.at[m], partner).wait_send()
            remote(land.at[:, lane(m)], land.at[:, lane(m)], ag_send.at[m], near_recv.at[m], partner).wait_send()

        @pl.when(jnp.logical_not(is_hub))
        def _(m=m):
            sent = stage.at[lane(m)]
            remote(sent, sent, rs_send.at[m], rs_recv.at[m], partner).wait_send()

    @pl.when(t > 0)
    def _():
        halo.wait_send()

    top = peaks[...]
    remote(slots, slots, peak_send, peak_recv, partner).wait_recv()
    for n in range(tiles_n - 1):
        top = jnp.maximum(top, slots[n])
    top = jnp.max(top, axis=1, keepdims=True)
    for k in range(count):
        at = k % per_block
        peak_out[k // per_block:k // per_block + 1, at:at + 1] = top[k:k + 1]
    remote(slots, slots, peak_send, peak_recv, partner).wait_send()


def write_out(scores, peaks, scores_out, peaks_out, sem):
    copies = [pltpu.make_async_copy(scores, scores_out, sem.at[0]), pltpu.make_async_copy(peaks, peaks_out, sem.at[1])]
    for copy in copies:
        copy.start()
    for copy in copies:
        copy.wait()


def local(tiles, library, block_owner, block_clips, layer_order):
    layers, rows, cols = tiles.shape
    e = library.shape[-1]
    nr = rows // e
    assert cols == 3 * e
    blocks, per_block = block_clips.shape
    count = blocks * per_block
    slabs = count * layers
    lanes = slabs // 2
    assert layers == 2 and count % UNROLL == 0
    tiles_n = lax.axis_size("tile")
    smem = pl.BlockSpec(memory_space=pltpu.SMEM)
    vmem = pl.BlockSpec(memory_space=pltpu.VMEM)
    dma = pltpu.SemaphoreType.DMA
    lines = -(-count // 8) * 8
    operands = [library, tiles, *constants(e)]
    scores, peaks = pl.pallas_call(
        functools.partial(kernel, tiles_n),
        out_shape=(pltpu.VMEM((blocks, per_block, rows, cols), F32),
                   pltpu.VMEM((blocks, per_block), F32)),
        in_specs=[smem] * 3 + [pl.BlockSpec(memory_space=pltpu.HBM)] * 8,
        out_specs=(vmem, vmem),
        scratch_shapes=[
            pltpu.VMEM((nr, e, cols), F32),
            pltpu.VMEM((nr, layers, 2, 4, e, e), F32), pltpu.VMEM((count, layers, 2, 4, e, e), F32),
            pltpu.VMEM((count, 1, e), F32), pltpu.VMEM((lines, e), F32), pltpu.VMEM((count, 1, e), F32),
            pltpu.VMEM((tiles_n - 1, lines, e), F32),
            pltpu.VMEM((lanes, e, e), F32), pltpu.VMEM((tiles_n - 1, lanes, e // HUBS, e), F32),
            pltpu.VMEM((2, lanes, e, e), F32), pltpu.VMEM((layers, e, cols), F32),
            *[dma((count,))] * 7, dma, dma, dma, dma,
        ] + [pltpu.VMEM(a.shape, a.dtype) for a in operands] + [dma((len(operands),))],
        compiler_params=pltpu.CompilerParams(collective_id=0, has_side_effects=True, vmem_limit_bytes=64600000),
    )(block_owner, block_clips, layer_order, *operands)
    hbm = pl.BlockSpec(memory_space=pltpu.HBM)
    scores, peaks = (pltpu.with_memory_space_constraint(a, pltpu.VMEM) for a in (scores, peaks))
    return pl.pallas_call(
        write_out,
        out_shape=(jax.ShapeDtypeStruct(scores.shape, F32), jax.ShapeDtypeStruct(peaks.shape, F32)),
        in_specs=[vmem, vmem],
        out_specs=(hbm, hbm),
        scratch_shapes=[dma((2,))],
        compiler_params=pltpu.CompilerParams(vmem_limit_bytes=1024 * 1024),
    )(scores, peaks)


def solution(mesh):
    in_specs = (
        P(None, ("groups", "tile"), None),
        P("tile", None, None, None),
        P(),
        P(),
        P(("groups", "tile"), None),
    )
    out_specs = (P(None, None, ("groups", "tile"), None), P("groups", None))
    return jax.shard_map(local, mesh=mesh, in_specs=in_specs, out_specs=out_specs, check_vma=False)
```

```python
import functools
import math

import jax
import jax.numpy as jnp
import numpy as np
from jax import lax
from jax.experimental import pallas as pl
from jax.experimental.pallas import tpu as pltpu
from jax.sharding import PartitionSpec as P

F32 = jnp.float32
BF16 = jnp.bfloat16


def split(x):
    high = x.astype(BF16)
    return high, (x - high.astype(F32)).astype(BF16)


def mm(a, b):
    return jnp.dot(a, b, preferred_element_type=F32)


def transform_matrix(extent):
    span = 2 * extent
    odd = 2 * np.arange(extent)[:, None] + 1
    angle = (odd * np.arange(span)[None, :] % (2 * span)) * (math.pi / span)
    return np.concatenate([np.cos(angle), np.sin(angle)], axis=0).astype(np.float32)


def cyclic_matrix(extent):
    span = 2 * extent
    angle = (np.arange(extent)[:, None] * np.arange(span)[None, :] % span) * (2 * math.pi / span)
    cosine, sine = np.cos(angle), np.sin(angle)
    sine[0] = 1 - 2 * (np.arange(span) % 2)
    return np.concatenate([cosine, sine], axis=0).astype(np.float32)


def halves(matrix):
    high = matrix.astype(BF16)
    low = (matrix - high.astype(np.float32)).astype(BF16)
    return high, low


def constants(extent):
    forward = transform_matrix(extent)
    rings = [cyclic_matrix(extent), forward]
    fh, fl = halves(forward)
    row_left = np.concatenate([fh, fl, fh], axis=1)
    col_right = np.stack([np.stack(halves(np.ascontiguousarray(r.T))) for r in rings])
    bh, bl = halves(np.ascontiguousarray(forward[:, :extent].T) * np.float32(1.0 / extent))
    back_left = np.concatenate([bh, bh, bl], axis=1)
    back_right = np.stack([np.stack(halves(r * np.float32(0.5 / extent))) for r in rings])
    offset = np.arange(2 * extent)[None, :] - np.arange(extent)[:, None]
    band = ((offset >= 0) & (offset < extent)).astype(BF16)
    band_left = np.concatenate([band, band], axis=1)
    band_right = np.ascontiguousarray(band.T)
    return [jnp.asarray(c) for c in (row_left, col_right, back_left, back_right, band_left, band_right)]


class Transforms:
    def __init__(self, refs, shapes):
        self.__dict__.update(refs)
        self.layers, self.rows, self.cols, self.e, self.per_block, self.count = shapes
        self.span = 2 * self.e
        self.nc = self.cols // self.e
        self.entries = self.layers * self.e * self.e

    def special(self):
        return lax.broadcasted_iota(jnp.int32, (self.e, self.e), 1) == 0

    def combine(self, y, cyclic):
        e = self.e
        a, b = y[:e, :e], y[:e, e:]
        c, d = y[e:, :e], y[e:, e:]
        parts = a - d, b + c, a + d, c - b
        if cyclic:
            first = self.special()
            parts = [jnp.where(first, own, part) for own, part in zip((a, c, b, d), parts)]
        return parts

    def weights(self, matrix, ring, rows):
        return jnp.concatenate([matrix[ring, 0, :rows], matrix[ring, 0, :rows], matrix[ring, 1, :rows]], axis=0)

    def tile_of(self, b, window):
        e, squares = self.e, None
        for l in range(self.layers):
            x = window(self.layer_of[l])
            squares = x * x if squares is None else squares + x * x
            xh, xl = split(x)
            y = mm(self.row_left[...], jnp.concatenate([xh, xh, xl], axis=0))
            head, middle, tail = y[:, :e], y[:, e:2 * e], y[:, 2 * e:]
            mh, ml = split(middle)
            for ring, start in enumerate((head + tail, head - tail)):
                sh, sl = split(start)
                y = mm(jnp.concatenate([sh, mh, sl, ml, sh, mh], axis=1), self.weights(self.col_right, ring, 2 * e))
                for n, part in enumerate(self.combine(y, ring == 0)):
                    self.tile_parts[b, l, ring, n] = part
        sh, sl = split(squares)
        energy = mm(self.band_left[...], jnp.concatenate([sh, sl], axis=0))
        eh, el = split(energy)
        for c in range(self.nc):
            width = min(2, self.nc - c) * e
            at = slice(c * e, c * e + width)
            total = mm(eh[:, at], self.band_right[:width]) + mm(el[:, at], self.band_right[:width])
            self.inv[b, :, c * e:(c + 1) * e] = 1.0 / jnp.sqrt(total / self.entries + 1e-05)

    def clip_of(self, k, layer_at):
        e, span, row_left = self.e, self.span, self.row_left
        chosen = [layer_at(l) for l in range(self.layers)]
        total = sum(x * x for x in chosen)
        ch, cl = split(jnp.concatenate(chosen, axis=1))
        left = jnp.concatenate([row_left[:, n * span:n * span + e] for n in range(3)], axis=1)
        first = mm(left, jnp.concatenate([ch, ch, cl], axis=0))
        fh, fl = split(jnp.concatenate([first[:, l * e:(l + 1) * e] for l in range(self.layers)], axis=0))
        left = jnp.concatenate([fh, fl, fh], axis=1)
        for ring in range(2):
            y = mm(left, self.weights(self.col_right, ring, e))
            for l in range(self.layers):
                for n, part in enumerate(self.combine(y[l * span:(l + 1) * span], ring == 0)):
                    self.spectra[k, l, ring, n] = part
        mean = jnp.sum(total, keepdims=True) / self.entries
        self.scale[k] = jnp.broadcast_to(0.5 / (math.sqrt(self.entries) * jnp.sqrt(mean + 1e-05)), (1, e))

    def product_of(self, b, k, ring):
        u1 = u2 = v1 = v2 = None
        for l in range(self.layers):
            p1, p2, q1, q2 = (self.tile_parts[b, l, ring, n] for n in range(4))
            c1, c2, d1, d2 = (self.spectra[k, l, ring, n] for n in range(4))
            t = (p1 * c1 + p2 * c2, p2 * c1 - p1 * c2, q1 * d1 + q2 * d2, q2 * d1 - q1 * d2)
            if u1 is None:
                u1, u2, v1, v2 = t
            else:
                u1, u2, v1, v2 = u1 + t[0], u2 + t[1], v1 + t[2], v2 + t[3]
        parts = u1 + v1, u2 - v2, u2 + v2, v1 - u1
        if ring == 0:
            first = self.special()
            parts = [jnp.where(first, own, part) for own, part in zip((u1, v1, u2, v2), parts)]
        return jnp.concatenate([jnp.concatenate(parts[:2], axis=1), jnp.concatenate(parts[2:], axis=1)], axis=0)

    def rows_of(self, z):
        left = self.back_left
        zh, zl = split(z)
        return mm(left[...], jnp.concatenate([zh, zl, zh], axis=0))

    def inverse_of(self, items):
        e, rings = self.e, []
        for ring in range(2):
            wh, wl = zip(*(split(self.rows_of(self.product_of(b, k, ring))) for b, k in items))
            wh, wl = jnp.concatenate(wh, axis=0), jnp.concatenate(wl, axis=0)
            both = mm(jnp.concatenate([wh, wl], axis=0), self.back_right[ring, 0])
            rings.append(both[:len(items) * e] + both[len(items) * e:] + mm(wh, self.back_right[ring, 1]))
        for n, (b, k) in enumerate(items):
            scale = self.scale[k]
            best = self.peaks[k]
            for c in range(self.nc):
                even, odd = (r[n * e:(n + 1) * e, c % 2 * e:(c % 2 + 1) * e] for r in rings)
                out = (even + odd if c < 2 else even - odd) * (self.inv[b, :, c * e:(c + 1) * e] * scale)
                at = pl.ds(pl.multiple_of(b * e, e), e)
                self.scores[k // self.per_block, k % self.per_block, at, c * e:(c + 1) * e] = out
                best = jnp.maximum(best, jnp.max(out, axis=0, keepdims=True))
            self.peaks[k] = best


MESH = pl.DeviceIdType.MESH
PLANE = 4
HUBS = 2 * PLANE
UNROLL = 4


def kernel(tiles_n, owner, picks, order, *refs):
    sources = refs[:8]
    (scores, peak_out,
           inv, tile_parts, spectra, scale, peaks, best, slots,
           stage, land, full, halo_in,
           rs_send, rs_recv, ag_send, near_recv, far_recv, pair_send, pair_recv,
           halo_send, halo_recv, peak_send, peak_recv,
           library, tiles, row_left, col_right, back_left, back_right, band_left, band_right, load_sem) = refs[8:]
    loads = [pltpu.make_async_copy(a, b, load_sem.at[n]) for n, (a, b) in enumerate(zip(
        sources, (library, tiles, row_left, col_right, back_left, back_right, band_left, band_right)))]
    for load in loads:
        load.start()
    g = lax.axis_index("groups")
    t = lax.axis_index("tile")
    per_block = picks.shape[1]
    layers, rows, cols = tiles.shape
    e = library.shape[-1]
    nr = rows // e
    count = picks.shape[0] * per_block
    layer_of = [sum(jnp.where(order[0, l] == own, l, 0) for l in range(1, layers)) for own in range(layers)]
    work = Transforms(dict(row_left=row_left, col_right=col_right, back_left=back_left, back_right=back_right,
                           band_left=band_left, band_right=band_right, scores=scores, inv=inv,
                           tile_parts=tile_parts, spectra=spectra, scale=scale, peaks=best, layer_of=layer_of),
                      (layers, rows, cols, e, per_block, count))
    parity = lax.rem(g, 2)
    other_g = g + 1 - 2 * parity
    core = lax.rem(t, 2)
    partner = (g, t + 1 - 2 * core)
    first_hub = (tiles_n // PLANE // 2 - 1) * PLANE
    is_hub = jnp.logical_and(t >= first_hub, t < first_hub + HUBS)
    others = [(g, lax.rem(t + d, tiles_n)) for d in range(1, tiles_n)]

    barrier = pltpu.get_barrier_semaphore()

    def greet(target):
        pl.semaphore_signal(barrier, inc=1, device_id=target, device_id_type=MESH)

    @pl.when(is_hub)
    def _():
        for target in others:
            greet(target)

    for n in range(HUBS // 2):
        greet((other_g, first_hub + 2 * n + core))

    lanes = count * layers // 2
    width = lanes // count
    part = e // HUBS
    loads[0].wait()
    for j in range(lanes):
        slab = 2 * j + parity
        clip, layer = slab // layers, lax.rem(slab, layers)
        block, which = clip // per_block, lax.rem(clip, per_block)
        mask = jnp.where(owner[block] == t, 1.0, 0.0).astype(F32)
        stage[j] = library[picks[block, which], layer] * mask

    pl.semaphore_wait(barrier, jnp.where(is_hub, HUBS - 1 + tiles_n // 2, HUBS))

    def remote(src, dst, send, recv, target):
        return pltpu.make_async_remote_copy(src_ref=src, dst_ref=dst, send_sem=send, recv_sem=recv,
                                            device_id=target, device_id_type=MESH)

    def place(hub):
        at = lax.rem(hub, 2) * (HUBS // 2) + hub // 2
        return pl.ds(pl.multiple_of(at * part, part), part)

    def lane(m):
        return pl.ds(m * width, width)

    mine = pl.ds(pl.multiple_of(core * (e // 2), e // 2), e // 2)
    for m in range(count):
        for n in range(HUBS):
            hub = lax.rem(t + n, HUBS)
            target = first_hub + hub
            slot = lax.rem(t - target + tiles_n, tiles_n) - 1

            @pl.when(t != target)
            def _(m=m, hub=hub, target=target, slot=slot):
                remote(stage.at[lane(m), place(hub)], land.at[slot, lane(m)],
                       rs_send.at[m], rs_recv.at[m], (g, target)).start()

    @pl.when(t == tiles_n - 1)
    def _():
        halo_in[...] = jnp.zeros_like(halo_in)

    peaks[...] = jnp.full(peaks.shape, -jnp.inf, F32)
    best[...] = jnp.full(best.shape, -jnp.inf, F32)
    for load in loads[1:]:
        load.wait()
    def tile_block(b, carry):
        work.tile_of(b, lambda l: tiles[l, pl.ds(pl.multiple_of(b * e, e), 2 * e)])
        return carry

    lax.fori_loop(0, nr - 1, tile_block, 0)

    @pl.when(is_hub)
    def _():
        at = place(t - first_hub)
        for m in range(count):
            remote(land.at[:, lane(m)], land.at[:, lane(m)], rs_send.at[m], rs_recv.at[m], partner).wait_recv()
            total = stage[lane(m), at]
            for d in range(tiles_n - 1):
                total = total + land[d, lane(m)]
            full[parity, lane(m), at] = total
            piece = full.at[parity, lane(m), at]
            for n in range(1, tiles_n // 2):
                remote(piece, piece, ag_send.at[m], near_recv.at[m], (g, lax.rem(t + 2 * n, tiles_n))).start()
            for n in range(tiles_n // 2):
                remote(piece, piece, ag_send.at[m], far_recv.at[m], (other_g, lax.rem(t + 2 * n, tiles_n))).start()

    halo = remote(tiles.at[:, pl.ds(0, e)], halo_in, halo_send, halo_recv, (g, t - 1))
    def pair(m):
        return remote(full.at[:, lane(m), mine], full.at[:, lane(m), mine], pair_send.at[m], pair_recv.at[m], partner)

    def arrive(m):
        far = full.at[0, lane(m), mine]
        remote(far, far, ag_send.at[m], far_recv.at[m], partner).wait_recv()

        @pl.when(is_hub)
        def _():
            near = full.at[0, lane(m), pl.ds(0, e // 2 - part)]
            remote(near, near, ag_send.at[m], near_recv.at[m], partner).wait_recv()

        @pl.when(jnp.logical_not(is_hub))
        def _():
            remote(far, far, ag_send.at[m], near_recv.at[m], partner).wait_recv()

        pair(m).start()

    arrive(0)

    @pl.when(t > 0)
    def _():
        halo.start()

    for k in range(count):
        if k < count - 1:
            arrive(k + 1)
        pair(k).wait_recv()
        for b in range(nr - 1 if k else 0):
            work.inverse_of([(b, k - 1)])
        work.clip_of(k, lambda l: full[l, k])

    @pl.when(t < tiles_n - 1)
    def _():
        halo.wait_recv()
    work.tile_of(nr - 1, lambda l: jnp.concatenate([tiles[l, rows - e:], halo_in[l]], axis=0))
    for b in range(nr - 1):
        work.inverse_of([(b, count - 1)])
    for k in range(count):
        work.inverse_of([(nr - 1, k)])
    for k in range(count):
        peaks[k:k + 1] = best[k]

    copies = [remote(peaks, slots.at[n], peak_send, peak_recv, target) for n, target in enumerate(others)]
    for copy in copies:
        copy.start()
    for m in range(count):
        pair(m).wait_send()

        @pl.when(is_hub)
        def _(m=m):
            sent = stage.at[lane(m), pl.ds(0, e - part)]
            remote(sent, sent, rs_send.at[m], rs_recv.at[m], partner).wait_send()
            remote(land.at[:, lane(m)], land.at[:, lane(m)], ag_send.at[m], near_recv.at[m], partner).wait_send()

        @pl.when(jnp.logical_not(is_hub))
        def _(m=m):
            sent = stage.at[lane(m)]
            remote(sent, sent, rs_send.at[m], rs_recv.at[m], partner).wait_send()

    @pl.when(t > 0)
    def _():
        halo.wait_send()

    top = peaks[...]
    remote(slots, slots, peak_send, peak_recv, partner).wait_recv()
    for n in range(tiles_n - 1):
        top = jnp.maximum(top, slots[n])
    top = jnp.max(top, axis=1, keepdims=True)
    for k in range(count):
        at = k % per_block
        peak_out[k // per_block:k // per_block + 1, at:at + 1] = top[k:k + 1]
    remote(slots, slots, peak_send, peak_recv, partner).wait_send()


def write_out(scores, peaks, scores_out, peaks_out, sem):
    copies = [pltpu.make_async_copy(scores, scores_out, sem.at[0]), pltpu.make_async_copy(peaks, peaks_out, sem.at[1])]
    for copy in copies:
        copy.start()
    for copy in copies:
        copy.wait()


def local(tiles, library, block_owner, block_clips, layer_order):
    layers, rows, cols = tiles.shape
    e = library.shape[-1]
    nr = rows // e
    assert cols == 3 * e
    blocks, per_block = block_clips.shape
    count = blocks * per_block
    slabs = count * layers
    lanes = slabs // 2
    assert layers == 2 and count % UNROLL == 0
    tiles_n = lax.axis_size("tile")
    smem = pl.BlockSpec(memory_space=pltpu.SMEM)
    vmem = pl.BlockSpec(memory_space=pltpu.VMEM)
    dma = pltpu.SemaphoreType.DMA
    lines = -(-count // 8) * 8
    operands = [library, tiles, *constants(e)]
    scores, peaks = pl.pallas_call(
        functools.partial(kernel, tiles_n),
        out_shape=(pltpu.VMEM((blocks, per_block, rows, cols), F32),
                   pltpu.VMEM((blocks, per_block), F32)),
        in_specs=[smem] * 3 + [pl.BlockSpec(memory_space=pltpu.HBM)] * 8,
        out_specs=(vmem, vmem),
        scratch_shapes=[
            pltpu.VMEM((nr, e, cols), F32),
            pltpu.VMEM((nr, layers, 2, 4, e, e), F32), pltpu.VMEM((count, layers, 2, 4, e, e), F32),
            pltpu.VMEM((count, 1, e), F32), pltpu.VMEM((lines, e), F32), pltpu.VMEM((count, 1, e), F32),
            pltpu.VMEM((tiles_n - 1, lines, e), F32),
            pltpu.VMEM((lanes, e, e), F32), pltpu.VMEM((tiles_n - 1, lanes, e // HUBS, e), F32),
            pltpu.VMEM((2, lanes, e, e), F32), pltpu.VMEM((layers, e, cols), F32),
            *[dma((count,))] * 7, dma, dma, dma, dma,
        ] + [pltpu.VMEM(a.shape, a.dtype) for a in operands] + [dma((len(operands),))],
        compiler_params=pltpu.CompilerParams(collective_id=0, has_side_effects=True, vmem_limit_bytes=64600000),
    )(block_owner, block_clips, layer_order, *operands)
    hbm = pl.BlockSpec(memory_space=pltpu.HBM)
    scores, peaks = (pltpu.with_memory_space_constraint(a, pltpu.VMEM) for a in (scores, peaks))
    return pl.pallas_call(
        write_out,
        out_shape=(jax.ShapeDtypeStruct(scores.shape, F32), jax.ShapeDtypeStruct(peaks.shape, F32)),
        in_specs=[vmem, vmem],
        out_specs=(hbm, hbm),
        scratch_shapes=[dma((2,))],
        compiler_params=pltpu.CompilerParams(vmem_limit_bytes=1024 * 1024),
    )(scores, peaks)


def solution(mesh):
    in_specs = (
        P(None, ("groups", "tile"), None),
        P("tile", None, None, None),
        P(),
        P(),
        P(("groups", "tile"), None),
    )
    out_specs = (P(None, None, ("groups", "tile"), None), P("groups", None))
    return jax.shard_map(local, mesh=mesh, in_specs=in_specs, out_specs=out_specs, check_vma=False)
```
